128 devices in a mesh: fluid: 32 (over x, y, core), solid: 4 (over z).
Axes of the slice: x: 4, y: 4, z: 4, core: 2. Of those that a mesh axis runs over, the one named last changes fastest.
Arguments:
- rbf_blocks: bfloat16 [13312, 256, 256], P(('fluid', 'solid')), may hold values from -0.375 to 0.375
- fluid_traction: bfloat16 [13312, 768], P(('fluid', 'solid')), may hold values from -24 to 24
- fluid_mass: bfloat16 [13312, 768], P(('fluid', 'solid')), may hold values from 0.19921875 to 2
- route: int32 [13312, 1], P(('fluid', 'solid')), may hold values from 0 to 127; in each aligned block of 104 rows (0 to 103, 104 to 207, ...) at most 2 rows name the same one
- slot: int32 [13312], P(('fluid', 'solid')), may hold values from 0 to 7
- shell_inverse: bfloat16 [1024, 768, 768], P(('fluid', 'solid')), may hold values from -0.0078125 to 0.0078125
- robin_coef: float32 [1024, 768], P(('fluid', 'solid')), may hold values from 1 to 27
- shell_start: float32 [1024, 768], P(('fluid', 'solid')), may hold values from -3 to 3
Outputs:
- shell_displacement: float32 [1024, 768], P(('fluid', 'solid'))
- fluid_load: bfloat16 [13312, 768], P(('fluid', 'solid'))
- residual_norms: float32 [6], replicated
The draws below stay inside these ranges and needn't reach their ends.
Inputs may be any that keep to these rules, and one draw needn't show every extreme that they name: `route`: among the 104 blocks of one device at most 2 name the same owner device.
All inputs are finite; a program needn't handle non-finite values.
Results may differ from the reference program's by a relative error of at most 0.009.
Values may be sent and summed in bfloat16 or wider, within the bound.
No kernel may reach another device: no remote copies, remote signals or barrier semaphores. Data moves between devices by JAX's collectives and lax.ppermute only.
A program may use at most 128 MiB of HBM per device.

```python
import math
import jax
import jax.numpy as jnp
import numpy as np
from jax import lax

NODES = 256
FB_DEV = 104
SB_DEV = 8
ITERS = 6
CAP = 2
NFB = 13312
NSB = 1024
N_FLUID = 32
N_SOLID = 4
DEVICES = 128


def place_ends(drawn, key, least, top_value):
    spot = [jax.random.randint(jax.random.fold_in(key, axis), (), 0, length) for axis, length in enumerate(drawn.shape)]
    widest = drawn.shape.index(max(drawn.shape))
    beside = spot[:widest] + [(spot[widest] + 1) % drawn.shape[widest]] + spot[widest + 1:]
    return drawn.at[tuple(spot)].set(least).at[tuple(beside)].set(top_value)


def level_of(key, extent, cuts, least, largest):
    loudness, own = 1.0, jax.random.fold_in(key, 6)
    for position, shards_of in cuts:
        draws = jnp.exp(jax.random.uniform(jax.random.fold_in(own, position), (shards_of,), jnp.float32, least / len(cuts), largest / len(cuts)))
        loudness = loudness * jnp.repeat(draws, extent[position] // shards_of).reshape([-1 if axis == position else 1 for axis in range(len(extent))])
    return loudness


def routed_block(rng, own, number, rows, amount, top, limit, slope):
    order = jax.random.permutation(rng, amount)
    crowded, ordinary = load_shares(amount, rows * top, limit, slope, True), load_shares(amount, rows * top, limit, slope, False)
    places = jnp.arange(amount)

    def named(tallies, offset_by):
        used = int((tallies > 0).sum())
        fixed = max(1, used // 4)
        moved = fixed + (places - fixed + offset_by * (used - fixed)) % max(1, amount - fixed)
        return jnp.zeros((amount,), jnp.int32).at[order[jnp.where(places < fixed, places, moved)]].set(jnp.asarray(tallies, jnp.int32))

    tallies = jnp.where(number % 4 == 0, named(crowded, number // 4), named(ordinary, number - number // 4 - 1))
    mixed = jax.random.permutation(jax.random.fold_in(own, 3), amount)
    giver, taker = mixed[0:amount // 2 * 2:2], mixed[1:amount // 2 * 2:2]
    slack = jnp.minimum(tallies[giver] - 1, limit - tallies[taker]) // 2
    slack = jnp.where((giver == order[0]) | (taker == order[0]) | (tallies[taker] == 0), 0, jnp.maximum(slack, 0))
    moved = jax.random.randint(jax.random.fold_in(own, 4), (amount // 2,), 0, 1 << 20) % (slack + 1)
    tallies = tallies.at[giver].add(-moved).at[taker].add(moved)
    members = jnp.searchsorted(jnp.cumsum(tallies), jnp.arange(rows * top), side="right").astype(jnp.int32)
    listing = members.reshape(top, rows).T
    listing = listing[jax.random.permutation(jax.random.fold_in(own, 1), rows)]
    offset_by = jax.random.randint(jax.random.fold_in(own, 2), (rows, 1), 0, top)
    return jnp.take_along_axis(listing, (jnp.arange(top)[None, :] + offset_by) % top, axis=1)


def load_shares(amount, total, reach, lean, full):
    portions = [(1 << 20) // math.isqrt(standing ** lean) + 1 for standing in range(1, amount + 1)]
    largest = reach if full else min(reach, max(-(-total // amount), total * portions[0] // sum(portions)))
    least = 1 if total - largest >= amount - 1 else 0
    counts, rest = [largest] + [least] * (amount - 1), total - largest - least * (amount - 1)
    while rest > 0:
        free = [i for i in range(1, amount) if counts[i] < largest] or [i for i in range(1, amount) if counts[i] < reach]
        mass, left = sum([portions[i] for i in free]), rest
        for i in free:
            extra = min(reach - counts[i], max(1, left * portions[i] // mass), rest)
            counts[i] = counts[i] + extra
            rest = rest - extra
    return np.array(counts)


def noise(own_key, dims, scale, bound, split=(), kind=jnp.bfloat16):
    drawn = scale * jax.random.normal(own_key, dims, jnp.float32)
    if split:
        drawn = drawn * level_of(own_key, dims, split, -0.22, 0.18)
    return jnp.clip(drawn, -bound, bound).astype(kind)


def setup_inputs(seed: int = 0) -> dict:
    splits = jax.random.split(jax.random.key(seed), 9)
    rbf_blocks = noise(splits[0], (NFB, NODES, NODES), NODES ** -0.5, 0.375, ((0, 128),))
    fluid_traction = noise(splits[1], (NFB, 3 * NODES), 4.0, 24.0, ((0, 128),))
    fluid_mass = jnp.clip(jnp.exp(math.log(2.0) - 2.306499 * jax.random.uniform(splits[2], (NFB, 3 * NODES), jnp.float32) ** level_of(splits[2], (NFB, 3 * NODES), ((0, 128),), -0.2, 0.2)), 0.19921875, 2.0).astype(jnp.bfloat16)
    route_keys = jax.random.split(jax.random.fold_in(splits[3], 1), NFB // FB_DEV)
    route_turns = jax.random.permutation(jax.random.fold_in(splits[3], 3), NFB // FB_DEV)
    route = jax.vmap(lambda own, number: routed_block(jax.random.fold_in(splits[3], 2), own, number, FB_DEV, DEVICES, 1, CAP, 0))(route_keys, route_turns).reshape((NFB, 1))
    slot = place_ends(jax.random.randint(splits[4], (NFB,), 0, SB_DEV), jax.random.fold_in(splits[4], 1), 0, SB_DEV - 1).astype(jnp.int32)
    shell_inverse = noise(splits[5], (NSB, 3 * NODES, 3 * NODES), (3 * NODES * 64 * FB_DEV // SB_DEV) ** -0.5, 0.0078125, ((0, 128),))
    robin_coef = jnp.clip(jnp.exp(math.log(27.0) - 3.295837 * jax.random.uniform(splits[6], (NSB, 3 * NODES), jnp.float32) ** level_of(splits[6], (NSB, 3 * NODES), ((0, 128),), -0.2, 0.2)), 1.0, 27.0)
    shell_start = noise(splits[7], (NSB, 3 * NODES), 0.5, 3.0, ((0, 128),), jnp.float32)
    return {"rbf_blocks": rbf_blocks, "fluid_traction": fluid_traction, "fluid_mass": fluid_mass, "route": route, "slot": slot, "shell_inverse": shell_inverse, "robin_coef": robin_coef, "shell_start": shell_start}


RELAX = 0.3
EPSILON = 1e-06

def fluid_side(pieces):
    hblock, displaced, traction, massive = pieces
    hfloat = hblock.astype(jnp.float32)
    moved = jnp.einsum('bcj,bij->bci', displaced.reshape(-1, 3, NODES).astype(jnp.float32), hfloat).reshape(-1, 3 * NODES)
    load = (traction.astype(jnp.float32) - massive.astype(jnp.float32) * moved).astype(jnp.bfloat16)
    mapped = jnp.einsum('bci,bij->bcj', load.reshape(-1, 3, NODES).astype(jnp.float32), hfloat).reshape(-1, 3 * NODES)
    return (load, mapped.astype(jnp.bfloat16))

def shell_side(pieces):
    inverse, forcing = pieces
    return jnp.einsum('bi,bij->bj', forcing.astype(jnp.float32), inverse.astype(jnp.float32))

def least_squares(gram, target_side):
    order = gram.shape[0]
    lower = [[None] * order for _ in range(order)]
    for row in range(order):
        for column in range(row + 1):
            total = gram[row, column]
            for inner in range(column):
                total = total - lower[row][inner] * lower[column][inner]
            if row == column:
                lower[row][row] = jnp.sqrt(total)
            else:
                lower[row][column] = total / lower[column][column]
    middle = []
    for row in range(order):
        total = target_side[row]
        for inner in range(row):
            total = total - lower[row][inner] * middle[inner]
        middle.append(total / lower[row][row])
    result = [None] * order
    for row in reversed(range(order)):
        total = middle[row]
        for inner in range(row + 1, order):
            total = total - lower[inner][row] * result[inner]
        result[row] = total / lower[row][row]
    return jnp.stack(result)

def reference(rbf_blocks, fluid_traction, fluid_mass, route, slot, shell_inverse, robin_coef, shell_start):
    groups = N_FLUID * N_SOLID
    breadth = 3 * NODES
    shells_all = shell_start.shape[0]
    target = (route[:, 0] * SB_DEV + slot).astype(jnp.int32)
    rbf_grouped = rbf_blocks.reshape(groups, FB_DEV, NODES, NODES)
    traction_grouped = fluid_traction.reshape(groups, FB_DEV, breadth)
    mass_grouped = fluid_mass.reshape(groups, FB_DEV, breadth)
    inverse_grouped = shell_inverse.reshape(groups, SB_DEV, breadth, breadth)
    count = shells_all * breadth
    batching = min(16, groups)
    current = shell_start
    residuals = []
    images = []
    norms = []
    last_load = None
    for iteration in range(ITERS):
        displaced = current.astype(jnp.bfloat16)[target]
        loads, mapped = lax.map(fluid_side, (rbf_grouped, displaced.reshape(groups, FB_DEV, breadth), traction_grouped, mass_grouped), batch_size=batching)
        last_load = loads.reshape(-1, breadth)
        shell_load = jax.ops.segment_sum(mapped.reshape(-1, breadth).astype(jnp.float32), target, num_segments=shells_all)
        forcing = (shell_load + robin_coef * current).astype(jnp.bfloat16)
        image = lax.map(shell_side, (inverse_grouped, forcing.reshape(groups, SB_DEV, breadth)), batch_size=batching).reshape(shells_all, breadth)
        residual = image - current
        squares = jnp.sum(residual * residual)
        norms.append(jnp.sqrt(squares / count + EPSILON))
        residuals.append(residual)
        images.append(image)
        if iteration == 0:
            current = current + RELAX * residual
        else:
            changes = jnp.stack([(residuals[i + 1] - residuals[i]).reshape(-1) for i in range(iteration)])
            image_changes = jnp.stack([images[i + 1] - images[i] for i in range(iteration)])
            gram = jnp.dot(changes, changes.T, precision=lax.Precision.HIGHEST)
            rhs = jnp.dot(changes, residual.reshape(-1), precision=lax.Precision.HIGHEST)
            coefs = least_squares(gram, -rhs)
            current = image + jnp.tensordot(coefs, image_changes, axes=1, precision=lax.Precision.HIGHEST)
    return (current, last_load, jnp.stack(norms))
```

```python
import jax
import jax.numpy as jnp
from jax import lax
from jax.experimental import pallas as pl
from jax.experimental.pallas import tpu as pltpu
from jax.sharding import Mesh
from jax.sharding import PartitionSpec as P

ITERS = 6
FLUID_SOLID = ("fluid_0", "fluid_1", "fluid_2", "solid")
FLUID = ("fluid_0", "fluid_1", "fluid_2")

RELAX = 0.3
EPSILON = 1e-06

LANES = 128
RHS_AT = 5
SQUARES_AT = 10
PIECE = 32
ROWS = 16


def least_squares(gram, target_side):
    order = len(target_side)
    lower = [[None] * order for _ in range(order)]
    for row in range(order):
        for column in range(row + 1):
            total = gram[row][column]
            for inner in range(column):
                total = total - lower[row][inner] * lower[column][inner]
            if row == column:
                lower[row][row] = jnp.sqrt(total)
            else:
                lower[row][column] = total / lower[column][column]
    middle = []
    for row in range(order):
        total = target_side[row]
        for inner in range(row):
            total = total - lower[row][inner] * middle[inner]
        middle.append(total / lower[row][row])
    result = [None] * order
    for row in reversed(range(order)):
        total = middle[row]
        for inner in range(row + 1, order):
            total = total - lower[inner][row] * result[inner]
        result[row] = total / lower[row][row]
    return result


def spread_sums(line):
    whole = line + pltpu.roll(line, LANES - PIECE, 1) + pltpu.roll(line, LANES - 2 * PIECE, 1)
    row = lax.broadcasted_iota(jnp.int32, (ROWS, LANES), 0)
    lane = lax.broadcasted_iota(jnp.int32, (ROWS, LANES), 1)
    picked = jnp.where(row == lane, jnp.broadcast_to(whole, (ROWS, LANES)), 0.0)
    return jnp.broadcast_to(jnp.sum(picked, axis=1, keepdims=True), (ROWS, LANES))


def solve_coefficients(sums):
    order = len(sums)
    gram = [[sums[row][column : column + 1] for column in range(row + 1)] for row in range(order)]
    target_side = [-sums[-1][RHS_AT + i : RHS_AT + i + 1] for i in range(order)]
    return least_squares(gram, target_side)


def lane_chunks(breadth):
    return [slice(at, at + LANES) for at in range(0, breadth, LANES)]


def fluid_call(
    step_index, incoming, base, changes, sums, rbf_blocks, traction, massive, group, last
):
    blocks, nodes, _ = rbf_blocks.shape
    breadth = 3 * nodes
    steps = blocks // group
    halves = nodes // LANES
    n_changes = len(changes)
    n_sums = len(sums)
    solving = step_index >= 2
    keep = 0 < step_index < ITERS - 1

    def body(*refs):
        refs = list(refs)
        incoming_ref = refs.pop(0)
        base_ref = refs.pop(0) if step_index else None
        change_refs = [refs.pop(0) for _ in range(n_changes)]
        sum_refs = [refs.pop(0) for _ in range(n_sums)]
        rbf_ref, traction_ref, mass_ref = refs.pop(0), refs.pop(0), refs.pop(0)
        mapped_ref = refs.pop(0)
        load_ref = refs.pop(0) if last else None
        base_out = refs.pop(0) if keep else None
        sums_out = refs.pop(0) if step_index else None
        coefs_out = refs.pop(0) if step_index else None
        spread_ref, result_ref = refs.pop(0), refs.pop(0)
        kept_ref = refs.pop(0) if last else None
        step = pl.program_id(0)

        @pl.when(step == 0)
        def _():
            spread_ref[...] = jnp.zeros_like(spread_ref)
            coefs = []
            if step_index:
                fresh = spread_sums(incoming_ref[blocks : blocks + 1, breadth : breadth + LANES])
                sums_out[...] = fresh
                coefs_out[...] = jnp.zeros_like(coefs_out)
                if solving:
                    coefs = solve_coefficients([ref[...] for ref in sum_refs] + [fresh])
                    for i, coef in enumerate(coefs):
                        coefs_out[i : i + 1, :] = coef
            for at, cut in enumerate(lane_chunks(breadth)):
                change = incoming_ref[:blocks, cut]
                if step_index == 0:
                    shown = change
                elif step_index == 1:
                    shown = base_ref[:blocks, cut] + RELAX * change
                    base_out[:, cut] = base_ref[:blocks, cut] + change
                else:
                    run = base_ref[:blocks, cut] + change
                    if keep:
                        base_out[:, cut] = run
                    shown = run + coefs[-1] * change
                    for coef, ref in zip(coefs, change_refs):
                        shown = shown + coef * ref[:blocks, cut]
                component, half = divmod(at, halves)
                spread_ref[half, pl.ds(component, blocks, stride=8), :] = shown

        loads = []
        for block in range(group):
            rows = pl.ds(pl.multiple_of((step * group + block) * 8, 8), 8)
            shown = jnp.concatenate(
                [spread_ref[half, rows, :] for half in range(halves)], axis=1
            ).astype(jnp.bfloat16)
            moved = lax.dot_general(
                shown, rbf_ref[block], (((1,), (1,)), ((), ())), preferred_element_type=jnp.float32
            )
            here = slice(block * 8, block * 8 + 8)
            load = traction_ref[here, :] - mass_ref[here, :] * moved
            loads.append(load.astype(jnp.bfloat16))
        for block in range(group):
            rows = pl.ds(pl.multiple_of((step * group + block) * 8, 8), 8)
            result = jnp.dot(loads[block], rbf_ref[block], preferred_element_type=jnp.float32)
            for half in range(halves):
                lanes = slice(half * LANES, (half + 1) * LANES)
                result_ref[half, rows, :] = result[:, lanes]
                if last:
                    kept_ref[half, rows, :] = loads[block][:, lanes].astype(jnp.float32)

        @pl.when(step == steps - 1)
        def _():
            for at, cut in enumerate(lane_chunks(breadth)):
                component, half = divmod(at, halves)
                rows = pl.ds(component, blocks, stride=8)
                mapped_ref[:, cut] = result_ref[half, rows, :].astype(jnp.bfloat16)
                if last:
                    load_ref[:, cut] = kept_ref[half, rows, :].astype(jnp.bfloat16)

    def whole(array):
        return pl.BlockSpec(array.shape, lambda s: (0,) * array.ndim)

    small = [incoming] + ([base] if step_index else []) + list(changes) + list(sums)
    out_shape = [jax.ShapeDtypeStruct((blocks, breadth), jnp.bfloat16)]
    if last:
        out_shape.append(jax.ShapeDtypeStruct((blocks, breadth), jnp.bfloat16))
    if keep:
        out_shape.append(jax.ShapeDtypeStruct((blocks, breadth), jnp.float32))
    if step_index:
        out_shape += [jax.ShapeDtypeStruct((ROWS, LANES), jnp.float32)] * 2
    scratch = [pltpu.VMEM((halves, blocks * 8, LANES), jnp.float32)] * (3 if last else 2)
    out = pl.pallas_call(
        body,
        grid=(steps,),
        in_specs=[whole(a) for a in small]
        + [
            pl.BlockSpec((group, nodes, nodes), lambda s: (s, 0, 0)),
            pl.BlockSpec((group * 8, nodes), lambda s: (s, 0)),
            pl.BlockSpec((group * 8, nodes), lambda s: (s, 0)),
        ],
        out_specs=[whole(a) for a in out_shape],
        out_shape=out_shape,
        scratch_shapes=scratch,
        compiler_params=pltpu.CompilerParams(vmem_limit_bytes=24 * 2**20),
        name="fluid_side",
    )(*small, rbf_blocks, traction, massive)
    out = list(out)
    mapped = out.pop(0)
    load = out.pop(0) if last else None
    base_next = out.pop(0) if keep else None
    fresh, coefs = (out.pop(0), out.pop(0)) if step_index else (None, None)
    return mapped, load, base_next, fresh, coefs


def full_sum(array):
    return jnp.sum(jnp.sum(array, axis=0, keepdims=True), axis=1, keepdims=True)


def next_current(step_index, coef, current, residual, images, cut):
    if step_index == 1:
        return current[:, cut] + RELAX * residual[:, cut]
    moving = images[-1][:, cut]
    for i in range(len(images) - 1):
        moving = moving + coef[i : i + 1, :] * (images[i + 1][:, cut] - images[i][:, cut])
    return moving


def shell_call(step_index, loads, coefs, shown, residuals, images, start, robin_coef, shell_inverse):
    shells, breadth, _ = shell_inverse.shape
    history = step_index

    def body(*refs):
        refs = list(refs)
        load_ref = refs.pop(0)
        coef_ref = refs.pop(0) if step_index else None
        shown_ref = refs.pop(0)
        residual_refs = [refs.pop(0) for _ in range(history)]
        image_refs = [refs.pop(0) for _ in range(history)]
        start_ref, robin_ref, inverse_ref = refs.pop(0), refs.pop(0), refs.pop(0)
        message_ref, image_ref, residual_ref, run_ref = [refs.pop(0) for _ in range(4)]
        current_ref, forcing_ref = refs.pop(0), refs.pop(0)
        step = pl.program_id(0)

        @pl.when(step == 0)
        def _():
            for cut in lane_chunks(breadth):
                if step_index:
                    moving = next_current(
                        step_index,
                        coef_ref[...],
                        start_ref,
                        residual_refs[-1],
                        image_refs,
                        cut,
                    )
                else:
                    moving = start_ref[:, cut]
                current_ref[:, cut] = moving
                forcing_ref[:, cut] = load_ref[:, cut] + robin_ref[:, cut] * moving
            image_ref[...] = jnp.zeros_like(image_ref)

        product = jnp.dot(
            forcing_ref[...].astype(jnp.bfloat16),
            inverse_ref[0],
            preferred_element_type=jnp.float32,
        )
        mine = lax.broadcasted_iota(jnp.int32, (shells, breadth), 0) == step
        image_ref[...] = jnp.where(mine, product, image_ref[...])

        @pl.when(step == shells - 1)
        def _():
            image = image_ref[...]
            residual = image - current_ref[...]
            residual_ref[...] = residual
            lane = lax.broadcasted_iota(jnp.int32, (1, LANES), 1)
            line = jnp.where(lane == SQUARES_AT, full_sum(residual * residual), 0.0)
            if step_index:
                chain = [ref[...] for ref in residual_refs] + [residual]
                changes = [chain[i + 1] - chain[i] for i in range(step_index)]
                for i, change in enumerate(changes):
                    line = line + jnp.where(lane == i, full_sum(changes[-1] * change), 0.0)
                    line = line + jnp.where(
                        lane == RHS_AT + i, full_sum(change * residual), 0.0
                    )
            head = line.astype(jnp.bfloat16).astype(jnp.float32)
            rest = line - head
            middle = rest.astype(jnp.bfloat16).astype(jnp.float32)
            tail = (rest - middle).astype(jnp.bfloat16).astype(jnp.float32)
            pieces = head + pltpu.roll(middle, PIECE, 1) + pltpu.roll(tail, 2 * PIECE, 1)
            difference = (image - shown_ref[...]).astype(jnp.bfloat16)
            run_ref[...] = shown_ref[...] + difference.astype(jnp.float32)
            row = lax.broadcasted_iota(jnp.int32, (8, LANES), 0)
            lower = jnp.where(row == 0, jnp.broadcast_to(pieces, (8, LANES)), 0.0)
            zeros = jnp.zeros((8, breadth), jnp.float32)
            message_ref[:, :breadth] = jnp.concatenate(
                [difference.astype(jnp.float32), zeros], axis=0
            ).astype(jnp.bfloat16)
            message_ref[:, breadth:] = jnp.concatenate(
                [jnp.zeros((8, LANES), jnp.float32), lower], axis=0
            ).astype(jnp.bfloat16)

    def whole(array):
        return pl.BlockSpec(array.shape, lambda s: (0,) * array.ndim)

    small = (
        [loads]
        + ([coefs] if step_index else [])
        + [shown]
        + list(residuals)
        + list(images)
        + [start, robin_coef]
    )
    out_shape = [jax.ShapeDtypeStruct((ROWS, breadth + LANES), jnp.bfloat16)] + [
        jax.ShapeDtypeStruct((shells, breadth), jnp.float32)
    ] * 3
    return pl.pallas_call(
        body,
        grid=(shells,),
        in_specs=[whole(a) for a in small]
        + [pl.BlockSpec((1, breadth, breadth), lambda s: (s, 0, 0))],
        out_specs=[whole(a) for a in out_shape],
        out_shape=out_shape,
        scratch_shapes=[pltpu.VMEM((shells, breadth), jnp.float32)] * 2,
        compiler_params=pltpu.CompilerParams(vmem_limit_bytes=24 * 2**20),
        name="shell_side",
    )(*small, shell_inverse)


def closing_call(line, sums, images, count):
    shells, breadth = images[0].shape
    n_sums = len(sums)

    def body(*refs):
        refs = list(refs)
        line_ref = refs.pop(0)
        sum_refs = [refs.pop(0) for _ in range(n_sums)]
        image_refs = [refs.pop(0) for _ in range(len(images))]
        current_ref, norm_ref = refs
        fresh = spread_sums(line_ref[0:1, :])
        every = [ref[...] for ref in sum_refs] + [fresh]
        coefs = solve_coefficients(every[1:])
        for cut in lane_chunks(breadth):
            moving = image_refs[-1][:, cut]
            for i, coef in enumerate(coefs):
                moving = moving + coef * (image_refs[i + 1][:, cut] - image_refs[i][:, cut])
            current_ref[:, cut] = moving
        lane = lax.broadcasted_iota(jnp.int32, (1, LANES), 1)
        squares = jnp.zeros((1, LANES), jnp.float32)
        for i, part in enumerate(every):
            squares = jnp.where(lane == i, part[SQUARES_AT : SQUARES_AT + 1], squares)
        norm_ref[...] = jnp.sqrt(squares / count + EPSILON)

    return pl.pallas_call(
        body,
        out_shape=[
            jax.ShapeDtypeStruct((shells, breadth), jnp.float32),
            jax.ShapeDtypeStruct((1, LANES), jnp.float32),
        ],
        name="closing",
    )(line, *sums, *images)


def spread_components(array, blocks, nodes):
    wide = array.astype(jnp.float32).reshape(blocks, 3, nodes)
    return jnp.pad(wide, ((0, 0), (0, 5), (0, 0))).reshape(blocks * 8, nodes)


def per_device(
    rbf_blocks, fluid_traction, fluid_mass, route, slot, shell_inverse, robin_coef, shell_start
):
    devices = lax.axis_size(FLUID) * lax.axis_size("solid")
    blocks = rbf_blocks.shape[0]
    nodes = rbf_blocks.shape[1]
    breadth = 3 * nodes
    shells = shell_inverse.shape[0]
    capacity = max(2, 2 * blocks // devices)
    slots_all = devices * capacity
    count = shells * devices * breadth

    def transport(buffer):
        width = buffer.shape[1]
        moved = lax.all_to_all(
            buffer.reshape(devices, capacity, width),
            FLUID_SOLID,
            split_axis=0,
            concat_axis=0,
            tiled=True,
        )
        return moved.reshape(devices * capacity, width)

    destination = route[:, 0]
    block_order = jnp.arange(blocks, dtype=jnp.int32)
    earlier = (destination[:, None] == destination[None, :]) & (
        block_order[None, :] < block_order[:, None]
    )
    slot_rank = jnp.sum(earlier.astype(jnp.int32), axis=1)
    position = destination * capacity + slot_rank
    positions = jnp.arange(slots_all, dtype=jnp.int32)
    placing = positions[:, None] == position[None, :]
    place_out = placing.astype(jnp.bfloat16)
    place_in = (position[:, None] == positions[None, :]).astype(jnp.bfloat16)
    adding = (jnp.arange(8) == 0).astype(jnp.bfloat16) / capacity
    place_in = jnp.concatenate(
        [place_in, jnp.broadcast_to(adding[:, None], (8, slots_all)).astype(jnp.bfloat16)]
    )
    wanted = jnp.max(jnp.where(placing, slot[None, :] + 1, 0), axis=1) - 1
    asked = lax.all_to_all(
        wanted.reshape(devices, capacity), FLUID_SOLID, split_axis=0, concat_axis=0, tiled=True
    ).reshape(slots_all)
    shell_ids = jnp.arange(ROWS, dtype=jnp.int32)
    picking = (
        (asked[:, None] == shell_ids[None, :]) | (shell_ids[None, :] == shells)
    ).astype(jnp.bfloat16)
    collecting = (shell_ids[:shells, None] == asked[None, :]).astype(jnp.bfloat16)
    traction = spread_components(fluid_traction, blocks, nodes)
    massive = spread_components(fluid_mass, blocks, nodes)
    group = next(n for n in (8, 4, 2, 1) if blocks % n == 0)

    start_half = shell_start.astype(jnp.bfloat16)
    message = jnp.pad(start_half, ((0, ROWS - shells), (0, 0)))
    shown = start_half.astype(jnp.float32)
    base = None
    changes = []
    sums = []
    residuals = []
    images = []
    last_load = None
    for iteration in range(ITERS):
        outgoing = jnp.dot(picking, message, preferred_element_type=jnp.float32).astype(
            jnp.bfloat16
        )
        incoming = jnp.dot(
            place_in, transport(outgoing), preferred_element_type=jnp.float32
        )
        last = iteration == ITERS - 1
        mapped, load, base_next, fresh, coefs = fluid_call(
            iteration,
            incoming,
            base,
            changes[1:],
            sums[1:],
            rbf_blocks,
            traction,
            massive,
            group,
            last,
        )
        if iteration == 0:
            base = incoming
        else:
            changes.append(incoming)
            base = base_next
            sums.append(fresh)
        last_load = load
        sending = jnp.dot(place_out, mapped, preferred_element_type=jnp.float32).astype(
            jnp.bfloat16
        )
        arrived = transport(sending)
        shell_load = jnp.dot(collecting, arrived, preferred_element_type=jnp.float32)
        message, image, residual, shown = shell_call(
            iteration,
            shell_load,
            coefs,
            shown,
            residuals,
            images,
            shell_start,
            robin_coef,
            shell_inverse,
        )
        residuals.append(residual)
        images.append(image)
    ending = jnp.broadcast_to(
        message[shells : shells + 1, breadth:], (slots_all, LANES)
    )
    line = jnp.dot(place_in[blocks:], transport(ending), preferred_element_type=jnp.float32)
    current, norms = closing_call(line, sums, images, count)
    return (current, last_load, norms[0, :ITERS])


def solution(mesh):
    split = Mesh(
        mesh.devices.reshape(4, 4, 2, mesh.shape["solid"]),
        ("fluid_0", "fluid_1", "fluid_2", "solid"),
    )
    placed = (
        P(FLUID_SOLID, None, None),
        P(FLUID_SOLID, None),
        P(FLUID_SOLID, None),
        P(FLUID_SOLID, None),
        P(FLUID_SOLID),
        P(FLUID_SOLID, None, None),
        P(FLUID_SOLID, None),
        P(FLUID_SOLID, None),
    )
    return jax.shard_map(
        per_device,
        mesh=split,
        in_specs=placed,
        out_specs=(P(FLUID_SOLID, None), P(FLUID_SOLID, None), P()),
        check_vma=False,
    )
```

```python
import jax
import jax.numpy as jnp
from jax import lax
from jax.experimental import pallas as pl
from jax.experimental.pallas import tpu as pltpu
from jax.sharding import Mesh
from jax.sharding import PartitionSpec as P

ITERS = 6
FLUID_SOLID = ("fluid_0", "fluid_1", "fluid_2", "solid")
FLUID = ("fluid_0", "fluid_1", "fluid_2")

RELAX = 0.3
EPSILON = 1e-06
VMEM_LIMIT = 16 * 2**20

LANES = 128
TILE = 16
RHS_AT = 5
SQUARES_AT = 10
PIECE = 32
ROWS = 16


def least_squares(gram, target_side):
    order = len(target_side)
    lower = [[None] * order for _ in range(order)]
    for row in range(order):
        for column in range(row + 1):
            total = gram[row][column]
            for inner in range(column):
                total = total - lower[row][inner] * lower[column][inner]
            if row == column:
                lower[row][row] = jnp.sqrt(total)
            else:
                lower[row][column] = total / lower[column][column]
    middle = []
    for row in range(order):
        total = target_side[row]
        for inner in range(row):
            total = total - lower[row][inner] * middle[inner]
        middle.append(total / lower[row][row])
    result = [None] * order
    for row in reversed(range(order)):
        total = middle[row]
        for inner in range(row + 1, order):
            total = total - lower[inner][row] * result[inner]
        result[row] = total / lower[row][row]
    return result


def spread_sums(line):
    whole = line + pltpu.roll(line, LANES - PIECE, 1) + pltpu.roll(line, LANES - 2 * PIECE, 1)
    row = lax.broadcasted_iota(jnp.int32, (ROWS, LANES), 0)
    lane = lax.broadcasted_iota(jnp.int32, (ROWS, LANES), 1)
    picked = jnp.where(row == lane, jnp.broadcast_to(whole, (ROWS, LANES)), 0.0)
    return jnp.broadcast_to(jnp.sum(picked, axis=1, keepdims=True), (ROWS, LANES))


def solve_coefficients(sums):
    order = len(sums)
    gram = [[sums[row][column : column + 1] for column in range(row + 1)] for row in range(order)]
    target_side = [-sums[-1][RHS_AT + i : RHS_AT + i + 1] for i in range(order)]
    return least_squares(gram, target_side)


def vmem():
    return pl.BlockSpec(memory_space=pltpu.VMEM)


def fluid_call(places, collect, messages, sums, rbf_blocks, traction, massive, group, last):
    blocks, nodes, _ = rbf_blocks.shape
    rows_all = messages[0].shape[0]
    chunks = 3 * nodes // LANES
    halves = nodes // LANES
    sum_row = collect.shape[0] - ROWS
    k = len(messages) - 1
    n_sums = len(sums)
    fold = 256

    def body(*refs):
        refs = list(refs)
        place_ref, collect_ref = refs.pop(0), refs.pop(0)
        message_refs = [refs.pop(0) for _ in range(k + 1)]
        sum_refs = [refs.pop(0) for _ in range(n_sums)]
        rbf_ref, traction_ref, mass_ref = refs.pop(0), refs.pop(0), refs.pop(0)
        sending_ref = refs.pop(0)
        load_ref = refs.pop(0) if last else None
        sums_out, coefs_out = (refs.pop(0), refs.pop(0)) if k else (None, None)
        shown_ref, result_ref = refs.pop(0), refs.pop(0)
        kept_ref = refs.pop(0) if last else None

        weights = []
        if k:
            line = jnp.dot(
                collect_ref[sum_row:, :], message_refs[-1][...], preferred_element_type=jnp.float32
            )
            fresh = spread_sums(line[:1])
            sums_out[...] = fresh
            coefs_out[...] = jnp.zeros_like(coefs_out)
            weights = [RELAX]
            if k >= 2:
                coefs = solve_coefficients([ref[...] for ref in sum_refs] + [fresh])
                for i, coef in enumerate(coefs):
                    coefs_out[i : i + 1, :] = coef
                weights = [None] + [1.0 + coef for coef in coefs]

        def show(at, carry):
            rows = pl.ds(pl.multiple_of(at * fold, fold), fold)
            shown = message_refs[0][rows, :].astype(jnp.float32)
            for weight, ref in zip(weights, message_refs[1:]):
                change = ref[rows, :].astype(jnp.float32)
                shown = shown + (change if weight is None else weight * change)
            shown_ref[rows, :] = shown
            result_ref[rows, :] = jnp.zeros((fold, LANES), jnp.float32)
            return carry

        lax.fori_loop(0, rows_all // fold, show, 0)
        shown_ref[rows_all:, :] = jnp.zeros((TILE, LANES), jnp.float32)

        def contract(at, carry):
            loads, spots = [], []
            for inner in range(group):
                block = at * group + inner
                spot = place_ref[block]
                spots.append(spot)
                shown = jnp.concatenate(
                    [shown_ref[pl.ds(spot + half, 8, stride=halves), :] for half in range(halves)],
                    axis=1,
                ).astype(jnp.bfloat16)
                moved = lax.dot_general(
                    shown,
                    rbf_ref[block],
                    (((1,), (1,)), ((), ())),
                    preferred_element_type=jnp.float32,
                )
                rows = pl.ds(pl.multiple_of(block * 8, 8), 8)
                load = (traction_ref[rows, :] - mass_ref[rows, :] * moved).astype(jnp.bfloat16)
                loads.append(load)
                if last:
                    for half in range(halves):
                        lanes = slice(half * LANES, (half + 1) * LANES)
                        kept_ref[half, rows, :] = load[:, lanes].astype(jnp.float32)
            for inner in range(group):
                block = at * group + inner
                result = jnp.dot(
                    loads[inner], rbf_ref[block], preferred_element_type=jnp.float32
                )
                for half in range(halves):
                    result_ref[pl.ds(spots[inner] + half, 3, stride=halves), :] = result[
                        :3, half * LANES : (half + 1) * LANES
                    ]
            return carry

        lax.fori_loop(0, blocks // group, contract, 0)
        sending_ref[...] = result_ref[...].astype(jnp.bfloat16)
        if last:
            for at in range(chunks):
                component, half = divmod(at, halves)
                load_ref[:, at * LANES : (at + 1) * LANES] = kept_ref[
                    half, pl.ds(component, blocks, stride=8), :
                ].astype(jnp.bfloat16)

    out_shape = [jax.ShapeDtypeStruct((rows_all, LANES), jnp.bfloat16)]
    if last:
        out_shape.append(jax.ShapeDtypeStruct((blocks, 3 * nodes), jnp.bfloat16))
    if k:
        out_shape += [jax.ShapeDtypeStruct((ROWS, LANES), jnp.float32)] * 2
    scratch = [
        pltpu.VMEM((rows_all + TILE, LANES), jnp.float32),
        pltpu.VMEM((rows_all, LANES), jnp.float32),
    ]
    if last:
        scratch.append(pltpu.VMEM((halves, blocks * 8, LANES), jnp.float32))
    inputs = (collect, *messages, *sums, rbf_blocks, traction, massive)
    out = pl.pallas_call(
        body,
        in_specs=[pl.BlockSpec(memory_space=pltpu.SMEM)] + [vmem()] * len(inputs),
        out_specs=[vmem()] * len(out_shape),
        out_shape=out_shape,
        scratch_shapes=scratch,
        compiler_params=pltpu.CompilerParams(vmem_limit_bytes=VMEM_LIMIT),
        name="fluid_side",
    )(places, *inputs)
    out = list(out)
    sending = out.pop(0)
    load = out.pop(0) if last else None
    fresh, coefs = (out.pop(0), out.pop(0)) if k else (None, None)
    return sending, load, fresh, coefs


def full_sum(array):
    return jnp.sum(jnp.sum(array, axis=0, keepdims=True), axis=1, keepdims=True)


def shell_call(
    arrived, coefs, shown, residuals, images, start, robin_coef, collect, pick, shell_inverse, last
):
    shells, breadth, _ = shell_inverse.shape
    chunks = breadth // LANES
    height = chunks * shells
    k = len(images)

    def body(*refs):
        refs = list(refs)
        arrived_ref = refs.pop(0)
        coef_ref = refs.pop(0) if k else None
        shown_ref = refs.pop(0)
        residual_refs = [refs.pop(0) for _ in range(k)]
        image_refs = [refs.pop(0) for _ in range(k)]
        start_ref, robin_ref, collect_ref, pick_ref, inverse_ref = [refs.pop(0) for _ in range(5)]
        message_ref, image_out = refs.pop(0), refs.pop(0)
        residual_out, shown_out = (None, None) if last else (refs.pop(0), refs.pop(0))

        load = jnp.dot(
            collect_ref[:height, :], arrived_ref[...], preferred_element_type=jnp.float32
        )
        if k == 0:
            current = start_ref[...]
        elif k == 1:
            current = start_ref[...] + RELAX * residual_refs[0][...]
        else:
            current = image_refs[-1][...]
            for i in range(k - 1):
                current = current + coef_ref[i : i + 1, :] * (
                    image_refs[i + 1][...] - image_refs[i][...]
                )
        forcing = load + robin_ref[...] * current
        forcing = jnp.concatenate(
            [forcing[t * shells : (t + 1) * shells] for t in range(chunks)], axis=1
        ).astype(jnp.bfloat16)
        row = lax.broadcasted_iota(jnp.int32, (shells, breadth), 0)

        def contract(s, picked):
            product = jnp.dot(forcing, inverse_ref[s], preferred_element_type=jnp.float32)
            return jnp.where(row == s, product, picked)

        wide = lax.fori_loop(
            0, shells, contract, jnp.zeros((shells, breadth), jnp.float32), unroll=2
        )
        image = jnp.concatenate([wide[:, t * LANES : (t + 1) * LANES] for t in range(chunks)], axis=0)
        image_out[...] = image
        residual = image - current
        lane = lax.broadcasted_iota(jnp.int32, (1, LANES), 1)
        line = jnp.where(lane == SQUARES_AT, full_sum(residual * residual), 0.0)
        if k:
            chain = [ref[...] for ref in residual_refs] + [residual]
            changes = [chain[i + 1] - chain[i] for i in range(k)]
            for i, change in enumerate(changes):
                line = line + jnp.where(lane == i, full_sum(changes[-1] * change), 0.0)
                line = line + jnp.where(lane == RHS_AT + i, full_sum(change * residual), 0.0)
        head = line.astype(jnp.bfloat16).astype(jnp.float32)
        rest = line - head
        middle = rest.astype(jnp.bfloat16).astype(jnp.float32)
        tail = (rest - middle).astype(jnp.bfloat16).astype(jnp.float32)
        pieces = head + pltpu.roll(middle, PIECE, 1) + pltpu.roll(tail, 2 * PIECE, 1)
        if last:
            message_ref[...] = jnp.broadcast_to(pieces, message_ref.shape).astype(jnp.bfloat16)
            return
        residual_out[...] = residual
        difference = (image - shown_ref[...]).astype(jnp.bfloat16)
        shown_out[...] = shown_ref[...] + difference.astype(jnp.float32)
        first = lax.broadcasted_iota(jnp.int32, (ROWS, LANES), 0) == 0
        below = jnp.where(first, jnp.broadcast_to(pieces, (ROWS, LANES)), 0.0).astype(jnp.bfloat16)
        message_ref[...] = jnp.dot(
            pick_ref[...],
            jnp.concatenate([difference, below], axis=0),
            preferred_element_type=jnp.float32,
        ).astype(jnp.bfloat16)

    inputs = (
        [arrived]
        + ([coefs] if k else [])
        + [shown, *residuals, *images, start, robin_coef, collect, pick, shell_inverse]
    )
    own = jax.ShapeDtypeStruct((height, LANES), jnp.float32)
    if last:
        out_shape = [jax.ShapeDtypeStruct((ROWS, LANES), jnp.bfloat16), own]
    else:
        out_shape = [jax.ShapeDtypeStruct(arrived.shape, jnp.bfloat16), own, own, own]
    return pl.pallas_call(
        body,
        in_specs=[vmem()] * len(inputs),
        out_specs=[vmem()] * len(out_shape),
        out_shape=out_shape,
        compiler_params=pltpu.CompilerParams(vmem_limit_bytes=VMEM_LIMIT),
        name="shell_side",
    )(*inputs)


def closing_call(line, sums, images, shells, count):
    height = images[0].shape[0]
    chunks = height // shells
    n_sums = len(sums)

    def body(*refs):
        refs = list(refs)
        line_ref = refs.pop(0)
        sum_refs = [refs.pop(0) for _ in range(n_sums)]
        image_refs = [refs.pop(0) for _ in range(len(images))]
        current_ref, norm_ref = refs
        fresh = spread_sums(line_ref[0:1, :])
        every = [ref[...] for ref in sum_refs] + [fresh]
        coefs = solve_coefficients(every[1:])
        moving = image_refs[-1][...]
        for i, coef in enumerate(coefs):
            moving = moving + coef * (image_refs[i + 1][...] - image_refs[i][...])
        for t in range(chunks):
            current_ref[:, t * LANES : (t + 1) * LANES] = moving[t * shells : (t + 1) * shells]
        lane = lax.broadcasted_iota(jnp.int32, (1, LANES), 1)
        squares = jnp.zeros((1, LANES), jnp.float32)
        for i, part in enumerate(every):
            squares = jnp.where(lane == i, part[SQUARES_AT : SQUARES_AT + 1], squares)
        norm_ref[...] = jnp.sqrt(squares / count + EPSILON)

    return pl.pallas_call(
        body,
        out_shape=[
            jax.ShapeDtypeStruct((shells, chunks * LANES), jnp.float32),
            jax.ShapeDtypeStruct((1, LANES), jnp.float32),
        ],
        name="closing",
    )(line, *sums, *images)


def spread_components(array, blocks, nodes):
    wide = array.astype(jnp.float32).reshape(blocks, 3, nodes)
    return jnp.pad(wide, ((0, 0), (0, 5), (0, 0))).reshape(blocks * 8, nodes)


def by_chunks(array, shells):
    return array.reshape(shells, -1, LANES).transpose(1, 0, 2).reshape(-1, LANES)


def per_device(
    rbf_blocks, fluid_traction, fluid_mass, route, slot, shell_inverse, robin_coef, shell_start
):
    devices = lax.axis_size(FLUID) * lax.axis_size("solid")
    blocks = rbf_blocks.shape[0]
    nodes = rbf_blocks.shape[1]
    breadth = 3 * nodes
    chunks = breadth // LANES
    shells = shell_inverse.shape[0]
    height = chunks * shells
    capacity = 2
    count = shells * devices * breadth

    def exchange(array):
        return lax.all_to_all(array, FLUID_SOLID, split_axis=0, concat_axis=0, tiled=True)

    def transport(buffer):
        return exchange(buffer.reshape(devices, TILE, LANES)).reshape(devices * TILE, LANES)

    destination = route[:, 0]
    block_order = jnp.arange(blocks, dtype=jnp.int32)
    earlier = (destination[:, None] == destination[None, :]) & (
        block_order[None, :] < block_order[:, None]
    )
    slot_rank = jnp.sum(earlier.astype(jnp.int32), axis=1)
    position = destination * capacity + slot_rank
    positions = jnp.arange(devices * capacity, dtype=jnp.int32)
    placing = positions[:, None] == position[None, :]
    wanted = jnp.max(jnp.where(placing, slot[None, :] + 1, 0), axis=1) - 1
    asked = exchange(wanted.reshape(devices, capacity))
    places = destination * TILE + slot_rank * chunks

    order = jnp.arange(TILE, dtype=jnp.int32)[None, :]
    named = jnp.where(order < chunks, asked[:, :1], asked[:, 1:2])
    shows = jnp.where(
        (named >= 0) & (order < capacity * chunks), (order % chunks) * shells + named, -1
    )
    shows = jnp.where(order == capacity * chunks, height, shows).reshape(devices * TILE)
    stacked = jnp.arange(height + ROWS, dtype=jnp.int32)
    pick = (shows[:, None] == stacked[None, :]).astype(jnp.bfloat16)
    collect = (stacked[:, None] == shows[None, :]).astype(jnp.bfloat16)

    traction = spread_components(fluid_traction, blocks, nodes)
    massive = spread_components(fluid_mass, blocks, nodes)
    start = by_chunks(shell_start, shells)
    robin = by_chunks(robin_coef, shells)
    group = next(n for n in (8, 4, 2, 1) if blocks % n == 0)

    start_half = start.astype(jnp.bfloat16)
    shown = start_half.astype(jnp.float32)
    outgoing = jnp.dot(
        pick, jnp.pad(start_half, ((0, ROWS), (0, 0))), preferred_element_type=jnp.float32
    ).astype(jnp.bfloat16)
    messages = []
    sums = []
    residuals = []
    images = []
    last_load = None
    for iteration in range(ITERS):
        last = iteration == ITERS - 1
        messages.append(transport(outgoing))
        sending, last_load, fresh, coefs = fluid_call(
            places, collect, messages, sums[1:], rbf_blocks, traction, massive, group, last
        )
        if iteration:
            sums.append(fresh)
        made = shell_call(
            transport(sending),
            coefs,
            shown,
            residuals,
            images,
            start,
            robin,
            collect,
            pick,
            shell_inverse,
            last,
        )
        outgoing, image = made[:2]
        images.append(image)
        if not last:
            residuals.append(made[2])
            shown = made[3]
    ending = exchange(jnp.broadcast_to(outgoing[:1], (devices, 1, LANES)))
    line = jnp.sum(ending.astype(jnp.float32), axis=0)
    current, norms = closing_call(line, sums, images, shells, count)
    return (current, last_load, norms[0, :ITERS])


def solution(mesh):
    split = Mesh(
        mesh.devices.reshape(4, 4, 2, mesh.shape["solid"]),
        ("fluid_0", "fluid_1", "fluid_2", "solid"),
    )
    placed = (
        P(FLUID_SOLID, None, None),
        P(FLUID_SOLID, None),
        P(FLUID_SOLID, None),
        P(FLUID_SOLID, None),
        P(FLUID_SOLID),
        P(FLUID_SOLID, None, None),
        P(FLUID_SOLID, None),
        P(FLUID_SOLID, None),
    )
    return jax.shard_map(
        per_device,
        mesh=split,
        in_specs=placed,
        out_specs=(P(FLUID_SOLID, None), P(FLUID_SOLID, None), P()),
        check_vma=False,
    )
```

```python
import jax
import jax.numpy as jnp
from jax import lax
from jax.experimental import pallas as pl
from jax.experimental.pallas import tpu as pltpu
from jax.sharding import Mesh
from jax.sharding import PartitionSpec as P

ITERS = 6
FLUID_SOLID = ("fluid_0", "fluid_1", "fluid_2", "solid")
FLUID = ("fluid_0", "fluid_1", "fluid_2")

RELAX = 0.3
EPSILON = 1e-06
SMALL_LIMIT = 12 * 2**20
STREAM_LIMIT = 24 * 2**20

LANES = 128
RHS_AT = 5
SQUARES_AT = 10
PIECE = 32
ROWS = 16
FORTH = 14
BACK = 12
FOLD = 256
FLUID_STREAMS = 2
SHELL_STREAMS = 1


def least_squares(gram, target_side):
    order = len(target_side)
    lower = [[None] * order for _ in range(order)]
    for row in range(order):
        for column in range(row + 1):
            total = gram[row][column]
            for inner in range(column):
                total = total - lower[row][inner] * lower[column][inner]
            if row == column:
                lower[row][row] = jnp.sqrt(total)
            else:
                lower[row][column] = total / lower[column][column]
    middle = []
    for row in range(order):
        total = target_side[row]
        for inner in range(row):
            total = total - lower[row][inner] * middle[inner]
        middle.append(total / lower[row][row])
    result = [None] * order
    for row in reversed(range(order)):
        total = middle[row]
        for inner in range(row + 1, order):
            total = total - lower[inner][row] * result[inner]
        result[row] = total / lower[row][row]
    return result


def spread_sums(line):
    whole = line + pltpu.roll(line, LANES - PIECE, 1) + pltpu.roll(line, LANES - 2 * PIECE, 1)
    row = lax.broadcasted_iota(jnp.int32, (ROWS, LANES), 0)
    lane = lax.broadcasted_iota(jnp.int32, (ROWS, LANES), 1)
    picked = jnp.where(row == lane, jnp.broadcast_to(whole, (ROWS, LANES)), 0.0)
    return jnp.broadcast_to(jnp.sum(picked, axis=1, keepdims=True), (ROWS, LANES))


def solve_coefficients(sums):
    order = len(sums)
    gram = [[sums[row][column : column + 1] for column in range(row + 1)] for row in range(order)]
    target_side = [-sums[-1][RHS_AT + i : RHS_AT + i + 1] for i in range(order)]
    return least_squares(gram, target_side)


def vmem():
    return pl.BlockSpec(memory_space=pltpu.VMEM)


def fluid_call(places, add_up, messages, sums, rbf_blocks, traction, massive, stream, last):
    blocks, nodes, _ = rbf_blocks.shape
    rows_all = messages[0].shape[0]
    chunks = 3 * nodes // LANES
    halves = nodes // LANES
    rows_back = add_up.shape[1] // FORTH * BACK
    k = len(messages) - 1
    n_sums = len(sums)
    group = next(n for n in (26, 16, 8, 4, 2, 1) if blocks % n == 0)
    lag = min(group, 13)
    steps = blocks // group

    def body(*refs):
        refs = list(refs)
        place_ref, add_ref = refs.pop(0), refs.pop(0)
        message_refs = [refs.pop(0) for _ in range(k + 1)]
        sum_refs = [refs.pop(0) for _ in range(n_sums)]
        source_ref, traction_ref, mass_ref = refs.pop(0), refs.pop(0), refs.pop(0)
        sending_ref = refs.pop(0)
        load_ref = refs.pop(0) if last else None
        sums_out, coefs_out = (refs.pop(0), refs.pop(0)) if k else (None, None)
        shown_ref, result_ref = refs.pop(0), refs.pop(0)
        kept_ref = refs.pop(0) if last else None
        rbf_ref, landed = (refs.pop(0), refs.pop(0)) if stream else (source_ref, None)

        def piece(at):
            rows = pl.ds(at * group, group)
            return pltpu.make_async_copy(source_ref.at[rows], rbf_ref.at[rows], landed.at[at])

        if stream:
            for at in range(steps):
                piece(at).start()

        weights = []
        if k:
            line = jnp.dot(
                add_ref[...], message_refs[-1][...], preferred_element_type=jnp.float32
            )
            fresh = spread_sums(line[:1])
            sums_out[...] = fresh
            coefs_out[...] = jnp.zeros_like(coefs_out)
            weights = [RELAX]
            if k >= 2:
                coefs = solve_coefficients([ref[...] for ref in sum_refs] + [fresh])
                for i, coef in enumerate(coefs):
                    coefs_out[i : i + 1, :] = coef
                weights = [None] + [1.0 + coef for coef in coefs]

        def show(at, carry):
            rows = pl.ds(pl.multiple_of(at * FOLD, FOLD), FOLD)
            shown = message_refs[0][rows, :].astype(jnp.float32)
            for weight, ref in zip(weights, message_refs[1:]):
                change = ref[rows, :].astype(jnp.float32)
                shown = shown + (change if weight is None else weight * change)
            shown_ref[rows, :] = shown
            return carry

        lax.fori_loop(0, rows_all // FOLD, show, 0)
        shown_ref[rows_all:, :] = jnp.zeros((16, LANES), jnp.float32)
        result_ref[...] = jnp.zeros_like(result_ref)

        def load_of(block):
            spot = place_ref[0, block]
            shown = jnp.concatenate(
                [shown_ref[pl.ds(spot + half, 8, stride=halves), :] for half in range(halves)],
                axis=1,
            ).astype(jnp.bfloat16)
            moved = lax.dot_general(
                shown, rbf_ref[block], (((1,), (1,)), ((), ())), preferred_element_type=jnp.float32
            )
            rows = pl.ds(pl.multiple_of(block * 8, 8), 8)
            load = (traction_ref[rows, :] - mass_ref[rows, :] * moved).astype(jnp.bfloat16)
            if last:
                for half in range(halves):
                    lanes = slice(half * LANES, (half + 1) * LANES)
                    kept_ref[half, rows, :] = load[:, lanes].astype(jnp.float32)
            return load

        def map_back(block, load):
            spot = place_ref[1, block]
            result = jnp.dot(load, rbf_ref[block], preferred_element_type=jnp.float32)
            for half in range(halves):
                result_ref[pl.ds(spot + half, 3, stride=halves), :] = result[
                    :3, half * LANES : (half + 1) * LANES
                ]

        def contract(at, carry):
            if stream:
                piece(at).wait()
            first = at * group
            loads = {}
            for inner in range(group + lag):
                if inner < group:
                    loads[inner] = load_of(first + inner)
                if inner >= lag:
                    map_back(first + inner - lag, loads.pop(inner - lag))
            return carry

        lax.fori_loop(0, steps, contract, 0)
        sending_ref[...] = result_ref[...].astype(jnp.bfloat16)
        if last:
            for at in range(chunks):
                component, half = divmod(at, halves)
                load_ref[:, at * LANES : (at + 1) * LANES] = kept_ref[
                    half, pl.ds(component, blocks, stride=8), :
                ].astype(jnp.bfloat16)

    out_shape = [jax.ShapeDtypeStruct((rows_back, LANES), jnp.bfloat16)]
    if last:
        out_shape.append(jax.ShapeDtypeStruct((blocks, 3 * nodes), jnp.bfloat16))
    if k:
        out_shape += [jax.ShapeDtypeStruct((ROWS, LANES), jnp.float32)] * 2
    scratch = [
        pltpu.VMEM((rows_all + 16, LANES), jnp.float32),
        pltpu.VMEM((rows_back, LANES), jnp.float32),
    ]
    if last:
        scratch.append(pltpu.VMEM((halves, blocks * 8, LANES), jnp.float32))
    if stream:
        scratch += [
            pltpu.VMEM(rbf_blocks.shape, rbf_blocks.dtype),
            pltpu.SemaphoreType.DMA((steps,)),
        ]
    inputs = (add_up, *messages, *sums, rbf_blocks, traction, massive)
    in_specs = [vmem()] * len(inputs)
    if stream:
        rbf_blocks = pltpu.with_memory_space_constraint(rbf_blocks, pltpu.HBM)
        inputs = (add_up, *messages, *sums, rbf_blocks, traction, massive)
        in_specs[-3] = pl.BlockSpec(memory_space=pltpu.HBM)
    out = pl.pallas_call(
        body,
        in_specs=[pl.BlockSpec(memory_space=pltpu.SMEM)] + in_specs,
        out_specs=[vmem()] * len(out_shape),
        out_shape=out_shape,
        scratch_shapes=scratch,
        compiler_params=pltpu.CompilerParams(
            vmem_limit_bytes=STREAM_LIMIT if stream else SMALL_LIMIT
        ),
        name="fluid_side",
    )(places, *inputs)
    out = list(out)
    sending = out.pop(0)
    load = out.pop(0) if last else None
    fresh, coefs = (out.pop(0), out.pop(0)) if k else (None, None)
    return sending, load, fresh, coefs


def full_sum(array):
    return jnp.sum(jnp.sum(array, axis=0, keepdims=True), axis=1, keepdims=True)


def shell_call(
    arrived,
    coefs,
    shown,
    residuals,
    images,
    start,
    robin_coef,
    collect,
    pick,
    shell_inverse,
    stream,
    last,
):
    shells, breadth, _ = shell_inverse.shape
    chunks = breadth // LANES
    height = chunks * shells
    k = len(images)

    def body(*refs):
        refs = list(refs)
        arrived_ref = refs.pop(0)
        coef_ref = refs.pop(0) if k else None
        shown_ref = refs.pop(0)
        residual_refs = [refs.pop(0) for _ in range(k)]
        image_refs = [refs.pop(0) for _ in range(k)]
        start_ref, robin_ref, collect_ref, pick_ref, inverse_ref = [refs.pop(0) for _ in range(5)]
        message_ref, image_out = refs.pop(0), refs.pop(0)
        residual_out, shown_out = (None, None) if last else (refs.pop(0), refs.pop(0))
        near_ref, landed = refs if stream else (inverse_ref, None)
        copies = []
        if stream:
            for s in range(shells):
                copies.append(
                    pltpu.make_async_copy(inverse_ref.at[s], near_ref.at[s], landed.at[s])
                )
                copies[-1].start()

        load = jnp.dot(collect_ref[...], arrived_ref[...], preferred_element_type=jnp.float32)
        if k == 0:
            current = start_ref[...]
        elif k == 1:
            current = start_ref[...] + RELAX * residual_refs[0][...]
        else:
            current = image_refs[-1][...]
            for i in range(k - 1):
                current = current + coef_ref[i : i + 1, :] * (
                    image_refs[i + 1][...] - image_refs[i][...]
                )
        forcing = load + robin_ref[...] * current
        forcing = jnp.concatenate(
            [forcing[t * shells : (t + 1) * shells] for t in range(chunks)], axis=1
        ).astype(jnp.bfloat16)
        row = lax.broadcasted_iota(jnp.int32, (shells, breadth), 0)

        wide = jnp.zeros((shells, breadth), jnp.float32)
        for s in range(shells):
            if stream:
                copies[s].wait()
            product = jnp.dot(forcing, near_ref[s], preferred_element_type=jnp.float32)
            wide = jnp.where(row == s, product, wide)
        image = jnp.concatenate([wide[:, t * LANES : (t + 1) * LANES] for t in range(chunks)], axis=0)
        image_out[...] = image
        residual = image - current
        lane = lax.broadcasted_iota(jnp.int32, (1, LANES), 1)
        line = jnp.where(lane == SQUARES_AT, full_sum(residual * residual), 0.0)
        if k:
            chain = [ref[...] for ref in residual_refs] + [residual]
            changes = [chain[i + 1] - chain[i] for i in range(k)]
            for i, change in enumerate(changes):
                line = line + jnp.where(lane == i, full_sum(changes[-1] * change), 0.0)
                line = line + jnp.where(lane == RHS_AT + i, full_sum(change * residual), 0.0)
        head = line.astype(jnp.bfloat16).astype(jnp.float32)
        rest = line - head
        middle = rest.astype(jnp.bfloat16).astype(jnp.float32)
        tail = (rest - middle).astype(jnp.bfloat16).astype(jnp.float32)
        pieces = head + pltpu.roll(middle, PIECE, 1) + pltpu.roll(tail, 2 * PIECE, 1)
        if last:
            message_ref[...] = jnp.broadcast_to(pieces, message_ref.shape).astype(jnp.bfloat16)
            return
        residual_out[...] = residual
        difference = (image - shown_ref[...]).astype(jnp.bfloat16)
        shown_out[...] = shown_ref[...] + difference.astype(jnp.float32)
        first = lax.broadcasted_iota(jnp.int32, (ROWS, LANES), 0) == 0
        below = jnp.where(first, jnp.broadcast_to(pieces, (ROWS, LANES)), 0.0).astype(jnp.bfloat16)
        message_ref[...] = jnp.dot(
            pick_ref[...],
            jnp.concatenate([difference, below], axis=0),
            preferred_element_type=jnp.float32,
        ).astype(jnp.bfloat16)

    inputs = (
        [arrived]
        + ([coefs] if k else [])
        + [shown, *residuals, *images, start, robin_coef, collect, pick, shell_inverse]
    )
    own = jax.ShapeDtypeStruct((height, LANES), jnp.float32)
    if last:
        out_shape = [jax.ShapeDtypeStruct((ROWS, LANES), jnp.bfloat16), own]
    else:
        rows_out = pick.shape[0]
        out_shape = [jax.ShapeDtypeStruct((rows_out, LANES), jnp.bfloat16), own, own, own]
    in_specs = [vmem()] * len(inputs)
    scratch = []
    if stream:
        inputs[-1] = pltpu.with_memory_space_constraint(shell_inverse, pltpu.HBM)
        in_specs[-1] = pl.BlockSpec(memory_space=pltpu.HBM)
        scratch = [
            pltpu.VMEM(shell_inverse.shape, shell_inverse.dtype),
            pltpu.SemaphoreType.DMA((shells,)),
        ]
    return pl.pallas_call(
        body,
        in_specs=in_specs,
        out_specs=[vmem()] * len(out_shape),
        out_shape=out_shape,
        scratch_shapes=scratch,
        compiler_params=pltpu.CompilerParams(
            vmem_limit_bytes=STREAM_LIMIT if stream else SMALL_LIMIT
        ),
        name="shell_side",
    )(*inputs)


def closing_call(line, sums, images, shells, count):
    height = images[0].shape[0]
    chunks = height // shells
    n_sums = len(sums)

    def body(*refs):
        refs = list(refs)
        line_ref = refs.pop(0)
        sum_refs = [refs.pop(0) for _ in range(n_sums)]
        image_refs = [refs.pop(0) for _ in range(len(images))]
        current_ref, norm_ref = refs
        fresh = spread_sums(line_ref[0:1, :])
        every = [ref[...] for ref in sum_refs] + [fresh]
        coefs = solve_coefficients(every[1:])
        moving = image_refs[-1][...]
        for i, coef in enumerate(coefs):
            moving = moving + coef * (image_refs[i + 1][...] - image_refs[i][...])
        for t in range(chunks):
            current_ref[:, t * LANES : (t + 1) * LANES] = moving[t * shells : (t + 1) * shells]
        lane = lax.broadcasted_iota(jnp.int32, (1, LANES), 1)
        squares = jnp.zeros((1, LANES), jnp.float32)
        for i, part in enumerate(every):
            squares = jnp.where(lane == i, part[SQUARES_AT : SQUARES_AT + 1], squares)
        norm_ref[...] = jnp.sqrt(squares / count + EPSILON)

    return pl.pallas_call(
        body,
        out_shape=[
            jax.ShapeDtypeStruct((shells, chunks * LANES), jnp.float32),
            jax.ShapeDtypeStruct((1, LANES), jnp.float32),
        ],
        name="closing",
    )(line, *sums, *images)


def spread_components(array, blocks, nodes):
    wide = array.astype(jnp.float32).reshape(blocks, 3, nodes)
    return jnp.pad(wide, ((0, 0), (0, 5), (0, 0))).reshape(blocks * 8, nodes)


def by_chunks(array, shells):
    return array.reshape(shells, -1, LANES).transpose(1, 0, 2).reshape(-1, LANES)


def per_device(
    rbf_blocks, fluid_traction, fluid_mass, route, slot, shell_inverse, robin_coef, shell_start
):
    devices = lax.axis_size(FLUID) * lax.axis_size("solid")
    blocks = rbf_blocks.shape[0]
    nodes = rbf_blocks.shape[1]
    breadth = 3 * nodes
    chunks = breadth // LANES
    shells = shell_inverse.shape[0]
    height = chunks * shells
    capacity = 2
    count = shells * devices * breadth

    def exchange(array):
        return lax.all_to_all(array, FLUID_SOLID, split_axis=0, concat_axis=0, tiled=True)

    def transport(buffer, part):
        moved = exchange(buffer.reshape(devices, -1, part, LANES))
        return moved.reshape(-1, LANES)

    destination = route[:, 0]
    block_order = jnp.arange(blocks, dtype=jnp.int32)
    earlier = (destination[:, None] == destination[None, :]) & (
        block_order[None, :] < block_order[:, None]
    )
    slot_rank = jnp.sum(earlier.astype(jnp.int32), axis=1)
    position = destination * capacity + slot_rank
    positions = jnp.arange(devices * capacity, dtype=jnp.int32)
    placing = positions[:, None] == position[None, :]
    wanted = jnp.max(jnp.where(placing, slot[None, :] + 1, 0), axis=1) - 1
    asked = exchange(wanted.reshape(devices, capacity))
    places = jnp.stack(
        [destination * FORTH + slot_rank * chunks, destination * BACK + slot_rank * chunks]
    )

    stacked = jnp.arange(height + ROWS, dtype=jnp.int32)

    def shows(size):
        order = jnp.arange(size, dtype=jnp.int32)[None, :]
        named = jnp.where(order < chunks, asked[:, :1], asked[:, 1:2])
        rows = jnp.where(
            (named >= 0) & (order < capacity * chunks), (order % chunks) * shells + named, -1
        )
        return jnp.where(order == capacity * chunks, height, rows).reshape(-1)

    pick = (shows(FORTH)[:, None] == stacked[None, :]).astype(jnp.bfloat16)
    collect = (stacked[:height, None] == shows(BACK)[None, :]).astype(jnp.bfloat16)
    summed = jnp.arange(devices * FORTH, dtype=jnp.int32)[None, :] % FORTH == capacity * chunks
    add_up = jnp.broadcast_to(summed, (ROWS, devices * FORTH)).astype(jnp.bfloat16)

    traction = spread_components(fluid_traction, blocks, nodes)
    massive = spread_components(fluid_mass, blocks, nodes)
    start = by_chunks(shell_start, shells)
    robin = by_chunks(robin_coef, shells)

    start_half = start.astype(jnp.bfloat16)
    shown = start_half.astype(jnp.float32)
    outgoing = jnp.dot(
        pick, jnp.pad(start_half, ((0, ROWS), (0, 0))), preferred_element_type=jnp.float32
    ).astype(jnp.bfloat16)
    messages = []
    sums = []
    residuals = []
    images = []
    last_load = None
    for iteration in range(ITERS):
        last = iteration == ITERS - 1
        messages.append(transport(outgoing, 2))
        sending, last_load, fresh, coefs = fluid_call(
            places,
            add_up,
            messages,
            sums[1:],
            rbf_blocks,
            traction,
            massive,
            iteration < FLUID_STREAMS,
            last,
        )
        if iteration:
            sums.append(fresh)
        made = shell_call(
            transport(sending, 4),
            coefs,
            shown,
            residuals,
            images,
            start,
            robin,
            collect,
            pick,
            shell_inverse,
            iteration < SHELL_STREAMS,
            last,
        )
        outgoing, image = made[:2]
        images.append(image)
        if not last:
            residuals.append(made[2])
            shown = made[3]
    ending = exchange(jnp.broadcast_to(outgoing[:1], (devices, 1, LANES)))
    line = jnp.sum(ending.astype(jnp.float32), axis=0)
    current, norms = closing_call(line, sums, images, shells, count)
    return (current, last_load, norms[0, :ITERS])


def solution(mesh):
    split = Mesh(
        mesh.devices.reshape(4, 4, 2, mesh.shape["solid"]),
        ("fluid_0", "fluid_1", "fluid_2", "solid"),
    )
    placed = (
        P(FLUID_SOLID, None, None),
        P(FLUID_SOLID, None),
        P(FLUID_SOLID, None),
        P(FLUID_SOLID, None),
        P(FLUID_SOLID),
        P(FLUID_SOLID, None, None),
        P(FLUID_SOLID, None),
        P(FLUID_SOLID, None),
    )
    return jax.shard_map(
        per_device,
        mesh=split,
        in_specs=placed,
        out_specs=(P(FLUID_SOLID, None), P(FLUID_SOLID, None), P()),
        check_vma=False,
    )
```

```python
import jax
import jax.numpy as jnp
from jax import lax
from jax.experimental import pallas as pl
from jax.experimental.pallas import tpu as pltpu
from jax.sharding import Mesh
from jax.sharding import PartitionSpec as P

ITERS = 6
FLUID_SOLID = ("fluid_0", "fluid_1", "fluid_2", "solid")
FLUID = ("fluid_0", "fluid_1", "fluid_2")

RELAX = 0.3
EPSILON = 1e-06
SMALL_LIMIT = 12 * 2**20
STREAM_LIMIT = 24 * 2**20

LANES = 128
RHS_AT = 5
SQUARES_AT = 10
PIECE = 32
ROWS = 16
FORTH = 14
BACK = 12
FOLD = 256
FLUID_STREAMS = 2
SHELL_STREAMS = 1


def least_squares(gram, target_side):
    order = len(target_side)
    lower = [[None] * order for _ in range(order)]
    scale = []
    for row in range(order):
        for column in range(row + 1):
            total = gram[row][column]
            for inner in range(column):
                total = total - lower[row][inner] * lower[column][inner]
            if row == column:
                scale.append(1.0 / jnp.sqrt(total))
            else:
                lower[row][column] = total * scale[column]
    middle = []
    for row in range(order):
        total = target_side[row]
        for inner in range(row):
            total = total - lower[row][inner] * middle[inner]
        middle.append(total * scale[row])
    result = [None] * order
    for row in reversed(range(order)):
        total = middle[row]
        for inner in range(row + 1, order):
            total = total - lower[inner][row] * result[inner]
        result[row] = total * scale[row]
    return result


def spread_sums(line):
    whole = line + pltpu.roll(line, LANES - PIECE, 1) + pltpu.roll(line, LANES - 2 * PIECE, 1)
    row = lax.broadcasted_iota(jnp.int32, (ROWS, LANES), 0)
    lane = lax.broadcasted_iota(jnp.int32, (ROWS, LANES), 1)
    picked = jnp.where(row == lane, jnp.broadcast_to(whole, (ROWS, LANES)), 0.0)
    return jnp.broadcast_to(jnp.sum(picked, axis=1, keepdims=True), (ROWS, LANES))


def solve_coefficients(sums):
    order = len(sums)
    gram = [[sums[row][column : column + 1] for column in range(row + 1)] for row in range(order)]
    target_side = [-sums[-1][RHS_AT + i : RHS_AT + i + 1] for i in range(order)]
    return least_squares(gram, target_side)


def vmem():
    return pl.BlockSpec(memory_space=pltpu.VMEM)


def asking_call(route, slot, devices, chunks):
    blocks = slot.shape[1]

    def body(route_ref, slot_ref, wanted_ref, places_ref):
        line = route_ref[...].astype(jnp.float32)
        down = lax.broadcasted_iota(jnp.int32, (blocks, blocks), 0)
        across = lax.broadcasted_iota(jnp.int32, (blocks, blocks), 1)
        wide = jnp.broadcast_to(line, (blocks, blocks))
        column = jnp.sum(jnp.where(down == across, wide, 0.0), axis=1, keepdims=True)
        earlier = jnp.where((column == wide) & (down < across), 1.0, 0.0)
        rank = jnp.sum(earlier, axis=0, keepdims=True)
        peer = lax.broadcasted_iota(jnp.int32, (devices, blocks), 0).astype(jnp.float32)
        mine = peer == jnp.broadcast_to(line, (devices, blocks))
        number = slot_ref[...].astype(jnp.float32) + 1.0
        for q in range(2):
            named = jnp.broadcast_to(jnp.where(rank == q, number, 0.0), (devices, blocks))
            found = jnp.sum(jnp.where(mine, named, 0.0), axis=1, keepdims=True)
            wanted_ref[:, q : q + 1] = found.astype(jnp.int32) - 1
        places_ref[0:1, :] = (line * FORTH + rank * chunks).astype(jnp.int32)
        places_ref[1:2, :] = (line * BACK + rank * chunks).astype(jnp.int32)

    return pl.pallas_call(
        body,
        in_specs=[vmem()] * 2,
        out_specs=[vmem()] * 2,
        out_shape=[
            jax.ShapeDtypeStruct((devices, 2), jnp.int32),
            jax.ShapeDtypeStruct((2, blocks), jnp.int32),
        ],
        name="asking",
    )(route, slot)


def fluid_call(places, add_up, messages, sums, rbf_blocks, traction, massive, stream, last):
    blocks, nodes, _ = rbf_blocks.shape
    rows_all = messages[0].shape[0]
    chunks = 3 * nodes // LANES
    halves = nodes // LANES
    rows_back = add_up.shape[1] // FORTH * BACK
    k = len(messages) - 1
    n_sums = len(sums)
    group = next(n for n in (26, 16, 8, 4, 2, 1) if blocks % n == 0)
    lag = min(group, 13)
    steps = blocks // group
    pieces = [(at * group, group) for at in range(steps)]
    if blocks == 104:
        pieces = [(0, 8), (8, 16), (24, 24), (48, 28), (76, 28)]

    def body(*refs):
        refs = list(refs)
        place_ref, add_ref = refs.pop(0), refs.pop(0)
        message_refs = [refs.pop(0) for _ in range(k + 1)]
        sum_refs = [refs.pop(0) for _ in range(n_sums)]
        source_ref, traction_ref, mass_ref = refs.pop(0), refs.pop(0), refs.pop(0)
        sending_ref = refs.pop(0)
        load_ref = refs.pop(0) if last else None
        sums_out, coefs_out = (refs.pop(0), refs.pop(0)) if k else (None, None)
        shown_ref, result_ref = refs.pop(0), refs.pop(0)
        kept_ref = refs.pop(0) if last else None
        rbf_ref, landed = (refs.pop(0), refs.pop(0)) if stream else (source_ref, None)

        def piece(at):
            rows = pl.ds(*pieces[at])
            return pltpu.make_async_copy(source_ref.at[rows], rbf_ref.at[rows], landed.at[at])

        if stream:
            for at in range(len(pieces)):
                piece(at).start()

        weights = []
        if k:
            line = jnp.dot(
                add_ref[...], message_refs[-1][...], preferred_element_type=jnp.float32
            )
            fresh = spread_sums(line[:1])
            sums_out[...] = fresh
            coefs_out[...] = jnp.zeros_like(coefs_out)
            weights = [RELAX]
            if k >= 2:
                coefs = solve_coefficients([ref[...] for ref in sum_refs] + [fresh])
                for i, coef in enumerate(coefs):
                    coefs_out[i : i + 1, :] = coef
                weights = [None] + [1.0 + coef for coef in coefs]

        def show(at, carry):
            rows = pl.ds(pl.multiple_of(at * FOLD, FOLD), FOLD)
            shown = message_refs[0][rows, :].astype(jnp.float32)
            for weight, ref in zip(weights, message_refs[1:]):
                change = ref[rows, :].astype(jnp.float32)
                shown = shown + (change if weight is None else weight * change)
            shown_ref[rows, :] = shown
            return carry

        lax.fori_loop(0, rows_all // FOLD, show, 0)
        shown_ref[rows_all:, :] = jnp.zeros((16, LANES), jnp.float32)
        result_ref[...] = jnp.zeros_like(result_ref)

        def load_of(block):
            spot = place_ref[0, block]
            shown = jnp.concatenate(
                [shown_ref[pl.ds(spot + half, 8, stride=halves), :] for half in range(halves)],
                axis=1,
            ).astype(jnp.bfloat16)
            moved = lax.dot_general(
                shown, rbf_ref[block], (((1,), (1,)), ((), ())), preferred_element_type=jnp.float32
            )
            rows = pl.ds(pl.multiple_of(block * 8, 8), 8)
            load = (traction_ref[rows, :] - mass_ref[rows, :] * moved).astype(jnp.bfloat16)
            if last:
                for half in range(halves):
                    lanes = slice(half * LANES, (half + 1) * LANES)
                    kept_ref[half, rows, :] = load[:, lanes].astype(jnp.float32)
            return load

        def map_back(block, load):
            spot = place_ref[1, block]
            result = jnp.dot(load, rbf_ref[block], preferred_element_type=jnp.float32)
            for half in range(halves):
                result_ref[pl.ds(spot + half, 3, stride=halves), :] = result[
                    :3, half * LANES : (half + 1) * LANES
                ]

        def contract(first, amount, behind):
            loads = {}
            for inner in range(amount + behind):
                if inner < amount:
                    loads[inner] = load_of(first + inner)
                if inner >= behind:
                    map_back(first + inner - behind, loads.pop(inner - behind))

        def contract_group(at, carry):
            contract(at * group, group, lag)
            return carry

        if stream:
            for at, (first, amount) in enumerate(pieces):
                piece(at).wait()
                contract(first, amount, min(amount, lag))
        else:
            lax.fori_loop(0, steps, contract_group, 0)
        sending_ref[...] = result_ref[...].astype(jnp.bfloat16)
        if last:
            for at in range(chunks):
                component, half = divmod(at, halves)
                load_ref[:, at * LANES : (at + 1) * LANES] = kept_ref[
                    half, pl.ds(component, blocks, stride=8), :
                ].astype(jnp.bfloat16)

    out_shape = [jax.ShapeDtypeStruct((rows_back, LANES), jnp.bfloat16)]
    if last:
        out_shape.append(jax.ShapeDtypeStruct((blocks, 3 * nodes), jnp.bfloat16))
    if k:
        out_shape += [jax.ShapeDtypeStruct((ROWS, LANES), jnp.float32)] * 2
    scratch = [
        pltpu.VMEM((rows_all + 16, LANES), jnp.float32),
        pltpu.VMEM((rows_back, LANES), jnp.float32),
    ]
    if last:
        scratch.append(pltpu.VMEM((halves, blocks * 8, LANES), jnp.float32))
    if stream:
        scratch += [
            pltpu.VMEM(rbf_blocks.shape, rbf_blocks.dtype),
            pltpu.SemaphoreType.DMA((len(pieces),)),
        ]
    inputs = (add_up, *messages, *sums, rbf_blocks, traction, massive)
    in_specs = [vmem()] * len(inputs)
    if stream:
        rbf_blocks = pltpu.with_memory_space_constraint(rbf_blocks, pltpu.HBM)
        inputs = (add_up, *messages, *sums, rbf_blocks, traction, massive)
        in_specs[-3] = pl.BlockSpec(memory_space=pltpu.HBM)
    out = pl.pallas_call(
        body,
        in_specs=[pl.BlockSpec(memory_space=pltpu.SMEM)] + in_specs,
        out_specs=[vmem()] * len(out_shape),
        out_shape=out_shape,
        scratch_shapes=scratch,
        compiler_params=pltpu.CompilerParams(
            vmem_limit_bytes=STREAM_LIMIT if stream else SMALL_LIMIT
        ),
        name="fluid_side",
    )(places, *inputs)
    out = list(out)
    sending = out.pop(0)
    load = out.pop(0) if last else None
    fresh, coefs = (out.pop(0), out.pop(0)) if k else (None, None)
    return sending, load, fresh, coefs


def full_sum(array):
    return jnp.sum(jnp.sum(array, axis=0, keepdims=True), axis=1, keepdims=True)


def shell_call(
    arrived,
    coefs,
    shown,
    residuals,
    images,
    start,
    robin_coef,
    collect,
    pick,
    shell_inverse,
    stream,
    last,
):
    shells, breadth, _ = shell_inverse.shape
    chunks = breadth // LANES
    height = chunks * shells
    k = len(images)

    def body(*refs):
        refs = list(refs)
        arrived_ref = refs.pop(0)
        coef_ref = refs.pop(0) if k else None
        shown_ref = refs.pop(0)
        residual_refs = [refs.pop(0) for _ in range(k)]
        image_refs = [refs.pop(0) for _ in range(k)]
        start_ref, robin_ref, collect_ref, pick_ref, inverse_ref = [refs.pop(0) for _ in range(5)]
        message_ref, image_out = refs.pop(0), refs.pop(0)
        residual_out, shown_out = (None, None) if last else (refs.pop(0), refs.pop(0))
        near_ref, landed = refs if stream else (inverse_ref, None)
        copies = []
        if stream:
            for s in range(shells):
                copies.append(
                    pltpu.make_async_copy(inverse_ref.at[s], near_ref.at[s], landed.at[s])
                )
                copies[-1].start()

        load = jnp.dot(collect_ref[...], arrived_ref[...], preferred_element_type=jnp.float32)
        if k == 0:
            current = start_ref[...]
        elif k == 1:
            current = start_ref[...] + RELAX * residual_refs[0][...]
        else:
            current = image_refs[-1][...]
            for i in range(k - 1):
                current = current + coef_ref[i : i + 1, :] * (
                    image_refs[i + 1][...] - image_refs[i][...]
                )
        forcing = load + robin_ref[...] * current
        forcing = jnp.concatenate(
            [forcing[t * shells : (t + 1) * shells] for t in range(chunks)], axis=1
        ).astype(jnp.bfloat16)
        row = lax.broadcasted_iota(jnp.int32, (shells, breadth), 0)

        wide = jnp.zeros((shells, breadth), jnp.float32)
        for s in range(shells):
            if stream:
                copies[s].wait()
            product = jnp.dot(forcing, near_ref[s], preferred_element_type=jnp.float32)
            wide = jnp.where(row == s, product, wide)
        image = jnp.concatenate([wide[:, t * LANES : (t + 1) * LANES] for t in range(chunks)], axis=0)
        image_out[...] = image
        residual = image - current
        lane = lax.broadcasted_iota(jnp.int32, (1, LANES), 1)
        line = jnp.where(lane == SQUARES_AT, full_sum(residual * residual), 0.0)
        if k:
            chain = [ref[...] for ref in residual_refs] + [residual]
            changes = [chain[i + 1] - chain[i] for i in range(k)]
            for i, change in enumerate(changes):
                line = line + jnp.where(lane == i, full_sum(changes[-1] * change), 0.0)
                line = line + jnp.where(lane == RHS_AT + i, full_sum(change * residual), 0.0)
        head = line.astype(jnp.bfloat16).astype(jnp.float32)
        rest = line - head
        middle = rest.astype(jnp.bfloat16).astype(jnp.float32)
        tail = (rest - middle).astype(jnp.bfloat16).astype(jnp.float32)
        pieces = head + pltpu.roll(middle, PIECE, 1) + pltpu.roll(tail, 2 * PIECE, 1)
        if last:
            message_ref[...] = jnp.broadcast_to(pieces, message_ref.shape).astype(jnp.bfloat16)
            return
        residual_out[...] = residual
        difference = (image - shown_ref[...]).astype(jnp.bfloat16)
        shown_out[...] = shown_ref[...] + difference.astype(jnp.float32)
        first = lax.broadcasted_iota(jnp.int32, (ROWS, LANES), 0) == 0
        below = jnp.where(first, jnp.broadcast_to(pieces, (ROWS, LANES)), 0.0).astype(jnp.bfloat16)
        message_ref[...] = jnp.dot(
            pick_ref[...],
            jnp.concatenate([difference, below], axis=0),
            preferred_element_type=jnp.float32,
        ).astype(jnp.bfloat16)

    inputs = (
        [arrived]
        + ([coefs] if k else [])
        + [shown, *residuals, *images, start, robin_coef, collect, pick, shell_inverse]
    )
    own = jax.ShapeDtypeStruct((height, LANES), jnp.float32)
    if last:
        out_shape = [jax.ShapeDtypeStruct((ROWS, LANES), jnp.bfloat16), own]
    else:
        rows_out = pick.shape[0]
        out_shape = [jax.ShapeDtypeStruct((rows_out, LANES), jnp.bfloat16), own, own, own]
    in_specs = [vmem()] * len(inputs)
    scratch = []
    if stream:
        inputs[-1] = pltpu.with_memory_space_constraint(shell_inverse, pltpu.HBM)
        in_specs[-1] = pl.BlockSpec(memory_space=pltpu.HBM)
        scratch = [
            pltpu.VMEM(shell_inverse.shape, shell_inverse.dtype),
            pltpu.SemaphoreType.DMA((shells,)),
        ]
    return pl.pallas_call(
        body,
        in_specs=in_specs,
        out_specs=[vmem()] * len(out_shape),
        out_shape=out_shape,
        scratch_shapes=scratch,
        compiler_params=pltpu.CompilerParams(
            vmem_limit_bytes=STREAM_LIMIT if stream else SMALL_LIMIT
        ),
        name="shell_side",
    )(*inputs)


def closing_call(ending, sums, images, shells, count):
    height = images[0].shape[0]
    chunks = height // shells
    n_sums = len(sums)

    def body(*refs):
        refs = list(refs)
        ending_ref = refs.pop(0)
        sum_refs = [refs.pop(0) for _ in range(n_sums)]
        image_refs = [refs.pop(0) for _ in range(len(images))]
        current_ref, norm_ref = refs
        pieces = jnp.sum(ending_ref[...].astype(jnp.float32), axis=0, keepdims=True)
        fresh = spread_sums(pieces * 0.5)
        every = [ref[...] for ref in sum_refs] + [fresh]
        coefs = solve_coefficients(every[1:])
        moving = image_refs[-1][...]
        for i, coef in enumerate(coefs):
            moving = moving + coef * (image_refs[i + 1][...] - image_refs[i][...])
        for t in range(chunks):
            current_ref[:, t * LANES : (t + 1) * LANES] = moving[t * shells : (t + 1) * shells]
        for i, part in enumerate(every):
            norm = jnp.sqrt(part[SQUARES_AT : SQUARES_AT + 1] / count + EPSILON)
            norm_ref[i] = norm[0, 0]

    return pl.pallas_call(
        body,
        in_specs=[vmem()] * (1 + n_sums + len(images)),
        out_specs=[vmem(), pl.BlockSpec(memory_space=pltpu.SMEM)],
        out_shape=[
            jax.ShapeDtypeStruct((shells, chunks * LANES), jnp.float32),
            jax.ShapeDtypeStruct((n_sums + 1,), jnp.float32),
        ],
        name="closing",
    )(ending, *sums, *images)


def spread_components(array, blocks, nodes):
    wide = array.astype(jnp.float32).reshape(blocks, 3, nodes)
    return jnp.pad(wide, ((0, 0), (0, 5), (0, 0))).reshape(blocks * 8, nodes)


def by_chunks(array, shells):
    return array.reshape(shells, -1, LANES).transpose(1, 0, 2).reshape(-1, LANES)


def per_device(
    rbf_blocks, fluid_traction, fluid_mass, route, slot, shell_inverse, robin_coef, shell_start
):
    devices = lax.axis_size(FLUID) * lax.axis_size("solid")
    blocks = rbf_blocks.shape[0]
    nodes = rbf_blocks.shape[1]
    breadth = 3 * nodes
    chunks = breadth // LANES
    shells = shell_inverse.shape[0]
    height = chunks * shells
    capacity = 2
    count = shells * devices * breadth

    def exchange(array):
        return lax.all_to_all(array, FLUID_SOLID, split_axis=0, concat_axis=0, tiled=True)

    def transport(buffer, part):
        moved = exchange(buffer.reshape(devices, -1, part, LANES))
        return moved.reshape(-1, LANES)

    start = by_chunks(shell_start, shells)
    start_half = start.astype(jnp.bfloat16)
    wanted, places = asking_call(
        route.reshape(1, blocks), slot.reshape(1, blocks), devices, chunks
    )
    asked = exchange(wanted.reshape(devices, 1, capacity)).reshape(devices, capacity)

    stacked = jnp.arange(height + ROWS, dtype=jnp.int32)

    def shows(size):
        order = jnp.arange(size, dtype=jnp.int32)[None, :]
        named = jnp.where(order < chunks, asked[:, :1], asked[:, 1:2])
        rows = jnp.where(
            (named >= 0) & (order < capacity * chunks), (order % chunks) * shells + named, -1
        )
        return jnp.where(order == capacity * chunks, height, rows).reshape(-1)

    pick = (shows(FORTH)[:, None] == stacked[None, :]).astype(jnp.bfloat16)
    collect = (stacked[:height, None] == shows(BACK)[None, :]).astype(jnp.bfloat16)
    summed = jnp.arange(devices * FORTH, dtype=jnp.int32)[None, :] % FORTH == capacity * chunks
    add_up = jnp.broadcast_to(summed, (ROWS, devices * FORTH)).astype(jnp.bfloat16)

    traction = spread_components(fluid_traction, blocks, nodes)
    massive = spread_components(fluid_mass, blocks, nodes)
    robin = by_chunks(robin_coef, shells)

    shown = start_half.astype(jnp.float32)
    outgoing = jnp.dot(
        pick, jnp.pad(start_half, ((0, ROWS), (0, 0))), preferred_element_type=jnp.float32
    ).astype(jnp.bfloat16)
    messages = []
    sums = []
    residuals = []
    images = []
    last_load = None
    for iteration in range(ITERS):
        last = iteration == ITERS - 1
        messages.append(transport(outgoing, 2))
        sending, last_load, fresh, coefs = fluid_call(
            places,
            add_up,
            messages,
            sums[1:],
            rbf_blocks,
            traction,
            massive,
            iteration < FLUID_STREAMS,
            last,
        )
        if iteration:
            sums.append(fresh)
        made = shell_call(
            transport(sending, 4),
            coefs,
            shown,
            residuals,
            images,
            start,
            robin,
            collect,
            pick,
            shell_inverse,
            iteration < SHELL_STREAMS,
            last,
        )
        outgoing, image = made[:2]
        images.append(image)
        if not last:
            residuals.append(made[2])
            shown = made[3]
    ending = transport(jnp.broadcast_to(outgoing[:1], (devices * 2, LANES)), 2)
    current, norms = closing_call(ending, sums, images, shells, count)
    return (current, last_load, norms)


def solution(mesh):
    split = Mesh(
        mesh.devices.reshape(4, 4, 2, mesh.shape["solid"]),
        ("fluid_0", "fluid_1", "fluid_2", "solid"),
    )
    placed = (
        P(FLUID_SOLID, None, None),
        P(FLUID_SOLID, None),
        P(FLUID_SOLID, None),
        P(FLUID_SOLID, None),
        P(FLUID_SOLID),
        P(FLUID_SOLID, None, None),
        P(FLUID_SOLID, None),
        P(FLUID_SOLID, None),
    )
    return jax.shard_map(
        per_device,
        mesh=split,
        in_specs=placed,
        out_specs=(P(FLUID_SOLID, None), P(FLUID_SOLID, None), P()),
        check_vma=False,
    )
```

```python
import jax
import jax.numpy as jnp
from jax import lax
from jax.experimental import pallas as pl
from jax.experimental.pallas import tpu as pltpu
from jax.sharding import Mesh
from jax.sharding import PartitionSpec as P

ITERS = 6
FLUID_SOLID = ("fluid_0", "fluid_1", "fluid_2", "solid")
FLUID = ("fluid_0", "fluid_1", "fluid_2")

RELAX = 0.3
EPSILON = 1e-06
SMALL_LIMIT = 12 * 2**20
STREAM_LIMIT = 24 * 2**20

LANES = 128
RHS_AT = 5
SQUARES_AT = 10
PIECE = 32
ROWS = 16
FORTH = 14
BACK = 12
FOLD = 256
FLUID_STREAMS = 2
SHELL_STREAMS = 2


def least_squares(gram, target_side):
    order = len(target_side)
    lower = [[None] * order for _ in range(order)]
    scale = []
    for row in range(order):
        for column in range(row + 1):
            total = gram[row][column]
            for inner in range(column):
                total = total - lower[row][inner] * lower[column][inner]
            if row == column:
                scale.append(1.0 / jnp.sqrt(total))
            else:
                lower[row][column] = total * scale[column]
    middle = []
    for row in range(order):
        total = target_side[row]
        for inner in range(row):
            total = total - lower[row][inner] * middle[inner]
        middle.append(total * scale[row])
    result = [None] * order
    for row in reversed(range(order)):
        total = middle[row]
        for inner in range(row + 1, order):
            total = total - lower[inner][row] * result[inner]
        result[row] = total * scale[row]
    return result


def spread_sums(line):
    whole = line + pltpu.roll(line, LANES - PIECE, 1) + pltpu.roll(line, LANES - 2 * PIECE, 1)
    row = lax.broadcasted_iota(jnp.int32, (ROWS, LANES), 0)
    lane = lax.broadcasted_iota(jnp.int32, (ROWS, LANES), 1)
    picked = jnp.where(row == lane, jnp.broadcast_to(whole, (ROWS, LANES)), 0.0)
    return jnp.broadcast_to(jnp.sum(picked, axis=1, keepdims=True), (ROWS, LANES))


def solve_coefficients(sums):
    order = len(sums)
    gram = [[sums[row][column : column + 1] for column in range(row + 1)] for row in range(order)]
    target_side = [-sums[-1][RHS_AT + i : RHS_AT + i + 1] for i in range(order)]
    return least_squares(gram, target_side)


def vmem():
    return pl.BlockSpec(memory_space=pltpu.VMEM)


def fluid_call(
    places, add_up, messages, sums, rbf_blocks, traction, massive, shells, stream, last
):
    blocks, nodes, _ = rbf_blocks.shape
    rows_all = messages[-1].shape[0]
    chunks = 3 * nodes // LANES
    halves = nodes // LANES
    k = len(messages) - 1
    first_time = k == 0
    devices = rows_all // (chunks * shells if first_time else FORTH)
    rows_back = devices * (FORTH if first_time else BACK)
    apart = shells if first_time else 1
    over = 16 * apart
    n_sums = len(sums)
    group = next(n for n in (26, 16, 8, 4, 2, 1) if blocks % n == 0)
    lag = min(group, 13)
    steps = blocks // group
    pieces = [(at * group, group) for at in range(steps)]
    if blocks == 104:
        pieces = [(0, 8), (8, 16), (24, 24), (48, 28), (76, 28)]

    def body(*refs):
        refs = list(refs)
        place_ref = refs.pop(0)
        add_ref = None if first_time else refs.pop(0)
        slot_ref = refs.pop(0) if first_time else None
        message_refs = [refs.pop(0) for _ in range(k + 1)]
        sum_refs = [refs.pop(0) for _ in range(n_sums)]
        source_ref, traction_ref, mass_ref = refs.pop(0), refs.pop(0), refs.pop(0)
        sending_ref = refs.pop(0)
        load_ref = refs.pop(0) if last else None
        start_out = refs.pop(0) if first_time else None
        sums_out, coefs_out = (refs.pop(0), refs.pop(0)) if k else (None, None)
        shown_ref, result_ref = refs.pop(0), refs.pop(0)
        kept_ref = refs.pop(0) if last else None
        begun_ref = refs.pop(0) if first_time else None
        rbf_ref, landed = (refs.pop(0), refs.pop(0)) if stream else (source_ref, None)

        def piece(at):
            rows = pl.ds(*pieces[at])
            return pltpu.make_async_copy(source_ref.at[rows], rbf_ref.at[rows], landed.at[at])

        if stream:
            for at in range(len(pieces)):
                piece(at).start()

        weights = []
        if k:
            line = jnp.dot(
                add_ref[...], message_refs[-1][...], preferred_element_type=jnp.float32
            )
            fresh = spread_sums(line[:1])
            sums_out[...] = fresh
            coefs_out[...] = jnp.zeros_like(coefs_out)
            weights = [RELAX]
            if k >= 2:
                coefs = solve_coefficients([ref[...] for ref in sum_refs] + [fresh])
                for i, coef in enumerate(coefs):
                    coefs_out[i : i + 1, :] = coef
                weights = [None] + [1.0 + coef for coef in coefs]

        def show(at, carry):
            rows = pl.ds(pl.multiple_of(at * FOLD, FOLD), FOLD)
            shown = message_refs[0][rows, :].astype(jnp.float32)
            for weight, ref in zip(weights, message_refs[1:]):
                change = ref[rows, :].astype(jnp.float32)
                shown = shown + (change if weight is None else weight * change)
            shown_ref[rows, :] = shown
            return carry

        lax.fori_loop(0, rows_all // FOLD, show, 0)
        shown_ref[rows_all:, :] = jnp.zeros((over, LANES), jnp.float32)
        result_ref[...] = jnp.zeros_like(result_ref)
        if first_time:
            begun_ref[...] = jnp.zeros_like(begun_ref)

        def load_of(block):
            spot = place_ref[0, block]
            rows = [
                shown_ref[pl.ds(spot + half * apart, 8, stride=halves * apart), :]
                for half in range(halves)
            ]
            if first_time:
                again = place_ref[2, block]
                for half in range(halves):
                    begun_ref[pl.ds(again + half, 3, stride=halves), :] = rows[half][:3]
            shown = jnp.concatenate(rows, axis=1).astype(jnp.bfloat16)
            moved = lax.dot_general(
                shown, rbf_ref[block], (((1,), (1,)), ((), ())), preferred_element_type=jnp.float32
            )
            rows = pl.ds(pl.multiple_of(block * 8, 8), 8)
            load = (traction_ref[rows, :] - mass_ref[rows, :] * moved).astype(jnp.bfloat16)
            if last:
                for half in range(halves):
                    lanes = slice(half * LANES, (half + 1) * LANES)
                    kept_ref[half, rows, :] = load[:, lanes].astype(jnp.float32)
            return load

        def map_back(block, load):
            spot = place_ref[1, block]
            result = jnp.dot(load, rbf_ref[block], preferred_element_type=jnp.float32)
            for half in range(halves):
                result_ref[pl.ds(spot + half, 3, stride=halves), :] = result[
                    :3, half * LANES : (half + 1) * LANES
                ]

        def contract(first, amount, behind):
            loads = {}
            for inner in range(amount + behind):
                if inner < amount:
                    loads[inner] = load_of(first + inner)
                if inner >= behind:
                    map_back(first + inner - behind, loads.pop(inner - behind))

        def contract_group(at, carry):
            contract(at * group, group, lag)
            return carry

        if stream:
            for at, (first, amount) in enumerate(pieces):
                piece(at).wait()
                contract(first, amount, min(amount, lag))
        else:
            lax.fori_loop(0, steps, contract_group, 0)
        if first_time:
            start_out[...] = begun_ref[...].astype(jnp.bfloat16)
            result_ref[pl.ds(2 * chunks, devices, stride=FORTH), :] = slot_ref[...]
        sending_ref[...] = result_ref[...].astype(jnp.bfloat16)
        if last:
            for at in range(chunks):
                component, half = divmod(at, halves)
                load_ref[:, at * LANES : (at + 1) * LANES] = kept_ref[
                    half, pl.ds(component, blocks, stride=8), :
                ].astype(jnp.bfloat16)

    out_shape = [jax.ShapeDtypeStruct((rows_back, LANES), jnp.bfloat16)]
    if last:
        out_shape.append(jax.ShapeDtypeStruct((blocks, 3 * nodes), jnp.bfloat16))
    if first_time:
        out_shape.append(jax.ShapeDtypeStruct((devices * FORTH, LANES), jnp.bfloat16))
    if k:
        out_shape += [jax.ShapeDtypeStruct((ROWS, LANES), jnp.float32)] * 2
    scratch = [
        pltpu.VMEM((rows_all + over, LANES), jnp.float32),
        pltpu.VMEM((rows_back, LANES), jnp.float32),
    ]
    if last:
        scratch.append(pltpu.VMEM((halves, blocks * 8, LANES), jnp.float32))
    if first_time:
        scratch.append(pltpu.VMEM((devices * FORTH, LANES), jnp.float32))
    if stream:
        scratch += [
            pltpu.VMEM(rbf_blocks.shape, rbf_blocks.dtype),
            pltpu.SemaphoreType.DMA((len(pieces),)),
        ]
    inputs = (add_up, *messages, *sums, rbf_blocks, traction, massive)
    in_specs = [vmem()] * len(inputs)
    if stream:
        rbf_blocks = pltpu.with_memory_space_constraint(rbf_blocks, pltpu.HBM)
        inputs = (add_up, *messages, *sums, rbf_blocks, traction, massive)
        in_specs[-3] = pl.BlockSpec(memory_space=pltpu.HBM)
    out = pl.pallas_call(
        body,
        in_specs=[pl.BlockSpec(memory_space=pltpu.SMEM)] + in_specs,
        out_specs=[vmem()] * len(out_shape),
        out_shape=out_shape,
        scratch_shapes=scratch,
        compiler_params=pltpu.CompilerParams(
            vmem_limit_bytes=STREAM_LIMIT if stream else SMALL_LIMIT
        ),
        name="fluid_side",
    )(places, *inputs)
    out = list(out)
    sending = out.pop(0)
    if first_time:
        return sending, out[0]
    load = out.pop(0) if last else None
    return sending, load, *out


def full_sum(array):
    return jnp.sum(jnp.sum(array, axis=0, keepdims=True), axis=1, keepdims=True)


def shell_call(
    arrived,
    coefs,
    shown,
    residuals,
    images,
    start,
    robin_coef,
    collect,
    pick,
    shell_inverse,
    stream,
    last,
):
    shells, breadth, _ = shell_inverse.shape
    chunks = breadth // LANES
    height = chunks * shells
    k = len(images)

    def body(*refs):
        refs = list(refs)
        arrived_ref = refs.pop(0)
        coef_ref = refs.pop(0) if k else None
        shown_ref = refs.pop(0)
        residual_refs = [refs.pop(0) for _ in range(k)]
        image_refs = [refs.pop(0) for _ in range(k)]
        start_ref, robin_ref, collect_ref, pick_ref, inverse_ref = [refs.pop(0) for _ in range(5)]
        message_ref, image_out = refs.pop(0), refs.pop(0)
        residual_out, shown_out = (None, None) if last else (refs.pop(0), refs.pop(0))
        near_ref, landed = refs if stream else (inverse_ref, None)
        copies = []
        if stream:
            for s in range(shells):
                copies.append(
                    pltpu.make_async_copy(inverse_ref.at[s], near_ref.at[s], landed.at[s])
                )
                copies[-1].start()

        load = jnp.dot(collect_ref[...], arrived_ref[...], preferred_element_type=jnp.float32)
        if k == 0:
            current = start_ref[...]
        elif k == 1:
            current = start_ref[...] + RELAX * residual_refs[0][...]
        else:
            current = image_refs[-1][...]
            for i in range(k - 1):
                current = current + coef_ref[i : i + 1, :] * (
                    image_refs[i + 1][...] - image_refs[i][...]
                )
        forcing = load + robin_ref[...] * current
        forcing = jnp.concatenate(
            [forcing[t * shells : (t + 1) * shells] for t in range(chunks)], axis=1
        ).astype(jnp.bfloat16)
        row = lax.broadcasted_iota(jnp.int32, (shells, breadth), 0)

        wide = jnp.zeros((shells, breadth), jnp.float32)
        for s in range(shells):
            if stream:
                copies[s].wait()
            product = jnp.dot(forcing, near_ref[s], preferred_element_type=jnp.float32)
            wide = jnp.where(row == s, product, wide)
        image = jnp.concatenate([wide[:, t * LANES : (t + 1) * LANES] for t in range(chunks)], axis=0)
        image_out[...] = image
        residual = image - current
        lane = lax.broadcasted_iota(jnp.int32, (1, LANES), 1)
        line = jnp.where(lane == SQUARES_AT, full_sum(residual * residual), 0.0)
        if k:
            chain = [ref[...] for ref in residual_refs] + [residual]
            changes = [chain[i + 1] - chain[i] for i in range(k)]
            for i, change in enumerate(changes):
                line = line + jnp.where(lane == i, full_sum(changes[-1] * change), 0.0)
                line = line + jnp.where(lane == RHS_AT + i, full_sum(change * residual), 0.0)
        head = line.astype(jnp.bfloat16).astype(jnp.float32)
        rest = line - head
        middle = rest.astype(jnp.bfloat16).astype(jnp.float32)
        tail = (rest - middle).astype(jnp.bfloat16).astype(jnp.float32)
        pieces = head + pltpu.roll(middle, PIECE, 1) + pltpu.roll(tail, 2 * PIECE, 1)
        if last:
            message_ref[...] = jnp.broadcast_to(pieces, message_ref.shape).astype(jnp.bfloat16)
            return
        residual_out[...] = residual
        difference = (image - shown_ref[...]).astype(jnp.bfloat16)
        shown_out[...] = shown_ref[...] + difference.astype(jnp.float32)
        first = lax.broadcasted_iota(jnp.int32, (ROWS, LANES), 0) == 0
        below = jnp.where(first, jnp.broadcast_to(pieces, (ROWS, LANES)), 0.0).astype(jnp.bfloat16)
        message_ref[...] = jnp.dot(
            pick_ref[...],
            jnp.concatenate([difference, below], axis=0),
            preferred_element_type=jnp.float32,
        ).astype(jnp.bfloat16)

    inputs = (
        [arrived]
        + ([coefs] if k else [])
        + [shown, *residuals, *images, start, robin_coef, collect, pick, shell_inverse]
    )
    own = jax.ShapeDtypeStruct((height, LANES), jnp.float32)
    if last:
        out_shape = [jax.ShapeDtypeStruct((ROWS, LANES), jnp.bfloat16), own]
    else:
        rows_out = pick.shape[0]
        out_shape = [jax.ShapeDtypeStruct((rows_out, LANES), jnp.bfloat16), own, own, own]
    in_specs = [vmem()] * len(inputs)
    scratch = []
    if stream:
        inputs[-1] = pltpu.with_memory_space_constraint(shell_inverse, pltpu.HBM)
        in_specs[-1] = pl.BlockSpec(memory_space=pltpu.HBM)
        scratch = [
            pltpu.VMEM(shell_inverse.shape, shell_inverse.dtype),
            pltpu.SemaphoreType.DMA((shells,)),
        ]
    return pl.pallas_call(
        body,
        in_specs=in_specs,
        out_specs=[vmem()] * len(out_shape),
        out_shape=out_shape,
        scratch_shapes=scratch,
        compiler_params=pltpu.CompilerParams(
            vmem_limit_bytes=STREAM_LIMIT if stream else SMALL_LIMIT
        ),
        name="shell_side",
    )(*inputs)


def closing_call(ending, sums, images, shells, count):
    height = images[0].shape[0]
    chunks = height // shells
    n_sums = len(sums)

    def body(*refs):
        refs = list(refs)
        ending_ref = refs.pop(0)
        sum_refs = [refs.pop(0) for _ in range(n_sums)]
        image_refs = [refs.pop(0) for _ in range(len(images))]
        current_ref, norm_ref = refs
        pieces = jnp.sum(ending_ref[...].astype(jnp.float32), axis=0, keepdims=True)
        fresh = spread_sums(pieces * 0.5)
        every = [ref[...] for ref in sum_refs] + [fresh]
        coefs = solve_coefficients(every[1:])
        moving = image_refs[-1][...]
        for i, coef in enumerate(coefs):
            moving = moving + coef * (image_refs[i + 1][...] - image_refs[i][...])
        for t in range(chunks):
            current_ref[:, t * LANES : (t + 1) * LANES] = moving[t * shells : (t + 1) * shells]
        for i, part in enumerate(every):
            norm = jnp.sqrt(part[SQUARES_AT : SQUARES_AT + 1] / count + EPSILON)
            norm_ref[i] = norm[0, 0]

    return pl.pallas_call(
        body,
        in_specs=[vmem()] * (1 + n_sums + len(images)),
        out_specs=[vmem(), pl.BlockSpec(memory_space=pltpu.SMEM)],
        out_shape=[
            jax.ShapeDtypeStruct((shells, chunks * LANES), jnp.float32),
            jax.ShapeDtypeStruct((n_sums + 1,), jnp.float32),
        ],
        name="closing",
    )(ending, *sums, *images)


def spread_components(array, blocks, nodes):
    wide = array.astype(jnp.float32).reshape(blocks, 3, nodes)
    return jnp.pad(wide, ((0, 0), (0, 5), (0, 0))).reshape(blocks * 8, nodes)


def by_chunks(array, shells):
    return array.reshape(shells, -1, LANES).transpose(1, 0, 2).reshape(-1, LANES)


def per_device(
    rbf_blocks, fluid_traction, fluid_mass, route, slot, shell_inverse, robin_coef, shell_start
):
    devices = lax.axis_size(FLUID) * lax.axis_size("solid")
    blocks = rbf_blocks.shape[0]
    nodes = rbf_blocks.shape[1]
    breadth = 3 * nodes
    chunks = breadth // LANES
    shells = shell_inverse.shape[0]
    height = chunks * shells
    capacity = 2
    count = shells * devices * breadth

    def exchange(array):
        return lax.all_to_all(array, FLUID_SOLID, split_axis=0, concat_axis=0, tiled=True)

    def transport(buffer, part):
        moved = exchange(buffer.reshape(devices, -1, part, LANES))
        return moved.reshape(-1, LANES)

    start = by_chunks(shell_start, shells)
    start_half = start.astype(jnp.bfloat16)

    destination = route[:, 0]
    block_order = jnp.arange(blocks, dtype=jnp.int32)
    earlier = (destination[:, None] == destination[None, :]) & (
        block_order[None, :] < block_order[:, None]
    )
    slot_rank = jnp.sum(earlier.astype(jnp.int32), axis=1)
    places = jnp.stack(
        [destination * FORTH + slot_rank * chunks, destination * BACK + slot_rank * chunks]
    )
    solid = lax.axis_size("solid")
    upper = destination // solid
    begun_from = upper % 2 * (devices // 2) + upper // 2 * solid + destination % solid
    first_places = jnp.stack(
        [
            begun_from * height + slot,
            destination * FORTH + slot_rank * chunks,
            destination * FORTH + slot_rank * chunks,
        ]
    )
    peers = jnp.arange(devices, dtype=jnp.int32)
    lanes = jnp.arange(LANES, dtype=jnp.int32)
    wanted = jnp.where(slot_rank[:, None] == lanes[None, :], slot[:, None] + 1, 0)
    asking = jnp.dot(
        (peers[:, None] == destination[None, :]).astype(jnp.bfloat16),
        wanted.astype(jnp.bfloat16),
        preferred_element_type=jnp.float32,
    )

    traction = spread_components(fluid_traction, blocks, nodes)
    massive = spread_components(fluid_mass, blocks, nodes)
    robin = by_chunks(robin_coef, shells)

    shown = start_half.astype(jnp.float32)
    stacked = jnp.arange(height + ROWS, dtype=jnp.int32)
    summed = jnp.arange(devices * FORTH, dtype=jnp.int32)[None, :] % FORTH == capacity * chunks
    add_up = jnp.broadcast_to(summed, (ROWS, devices * FORTH)).astype(jnp.bfloat16)

    def one_hot(asked):
        order = jnp.arange(FORTH, dtype=jnp.int32)[None, :]
        named = jnp.where(order < chunks, asked[:, :1], asked[:, 1:2])
        rows = jnp.where(
            (named >= 0) & (order < capacity * chunks), (order % chunks) * shells + named, -1
        )
        forth = jnp.where(order == capacity * chunks, height, rows).reshape(-1)
        pick = (forth[:, None] == stacked[None, :]).astype(jnp.bfloat16)
        collect_first = (stacked[:height, None] == rows.reshape(-1)[None, :]).astype(jnp.bfloat16)
        back = rows[:, :BACK].reshape(-1)
        collect = (stacked[:height, None] == back[None, :]).astype(jnp.bfloat16)
        return pick, collect_first, collect

    begun = start_half
    for axes, amount in ((("fluid_0", "fluid_1", "solid"), devices // 2), (("fluid_2",), 2)):
        begun = lax.all_to_all(
            jnp.broadcast_to(begun[None], (amount, *begun.shape)),
            axes,
            split_axis=0,
            concat_axis=0,
            tiled=True,
        ).reshape(-1, LANES)
    messages = []
    sums = []
    residuals = []
    images = []
    last_load = None
    for iteration in range(ITERS):
        last = iteration == ITERS - 1
        coefs = None
        if iteration == 0:
            sending, message = fluid_call(
                first_places, asking, [begun], [], rbf_blocks, traction, massive, shells, True, last
            )
            arrived = transport(sending, 2)
            asked = arrived.reshape(devices, FORTH, LANES)[:, capacity * chunks, :capacity]
            pick, collect_now, collect = one_hot(asked.astype(jnp.int32) - 1)
            pick, collect_now, collect, add_up, places, arrived = lax.optimization_barrier(
                (pick, collect_now, collect, add_up, places, arrived)
            )
        else:
            message = transport(outgoing, 2)
        messages.append(message)
        if iteration:
            sending, last_load, fresh, coefs = fluid_call(
                places,
                add_up,
                messages,
                sums[1:],
                rbf_blocks,
                traction,
                massive,
                shells,
                iteration < FLUID_STREAMS,
                last,
            )
            sums.append(fresh)
            arrived = transport(sending, 4)
            collect_now = collect
        made = shell_call(
            arrived,
            coefs,
            shown,
            residuals,
            images,
            start,
            robin,
            collect_now,
            pick,
            shell_inverse,
            iteration < SHELL_STREAMS,
            last,
        )
        outgoing, image = made[:2]
        images.append(image)
        if not last:
            residuals.append(made[2])
            shown = made[3]
    ending = transport(jnp.broadcast_to(outgoing[:1], (devices * 2, LANES)), 2)
    current, norms = closing_call(ending, sums, images, shells, count)
    return (current, last_load, norms)


def solution(mesh):
    split = Mesh(
        mesh.devices.reshape(4, 4, 2, mesh.shape["solid"]),
        ("fluid_0", "fluid_1", "fluid_2", "solid"),
    )
    placed = (
        P(FLUID_SOLID, None, None),
        P(FLUID_SOLID, None),
        P(FLUID_SOLID, None),
        P(FLUID_SOLID, None),
        P(FLUID_SOLID),
        P(FLUID_SOLID, None, None),
        P(FLUID_SOLID, None),
        P(FLUID_SOLID, None),
    )
    return jax.shard_map(
        per_device,
        mesh=split,
        in_specs=placed,
        out_specs=(P(FLUID_SOLID, None), P(FLUID_SOLID, None), P()),
        check_vma=False,
    )
```

```python
import jax
import jax.numpy as jnp
from jax import lax
from jax.experimental import pallas as pl
from jax.experimental.pallas import tpu as pltpu
from jax.sharding import Mesh
from jax.sharding import PartitionSpec as P

ITERS = 6
FLUID_SOLID = ("fluid_0", "fluid_1", "fluid_2", "solid")
FLUID = ("fluid_0", "fluid_1", "fluid_2")

RELAX = 0.3
EPSILON = 1e-06
SMALL_LIMIT = 12 * 2**20
STREAM_LIMIT = 24 * 2**20

LANES = 128
RHS_AT = 5
SQUARES_AT = 10
PIECE = 32
ROWS = 16
FORTH = 14
BACK = 12
FOLD = 256
FLUID_STREAMS = 2
SHELL_STREAMS = 2


def least_squares(gram, target_side):
    order = len(target_side)
    lower = [[None] * order for _ in range(order)]
    scale = []
    for row in range(order):
        for column in range(row + 1):
            total = gram[row][column]
            for inner in range(column):
                total = total - lower[row][inner] * lower[column][inner]
            if row == column:
                scale.append(1.0 / jnp.sqrt(total))
            else:
                lower[row][column] = total * scale[column]
    middle = []
    for row in range(order):
        total = target_side[row]
        for inner in range(row):
            total = total - lower[row][inner] * middle[inner]
        middle.append(total * scale[row])
    result = [None] * order
    for row in reversed(range(order)):
        total = middle[row]
        for inner in range(row + 1, order):
            total = total - lower[inner][row] * result[inner]
        result[row] = total * scale[row]
    return result


def spread_sums(line):
    whole = line + pltpu.roll(line, LANES - PIECE, 1) + pltpu.roll(line, LANES - 2 * PIECE, 1)
    row = lax.broadcasted_iota(jnp.int32, (ROWS, LANES), 0)
    lane = lax.broadcasted_iota(jnp.int32, (ROWS, LANES), 1)
    picked = jnp.where(row == lane, jnp.broadcast_to(whole, (ROWS, LANES)), 0.0)
    return jnp.broadcast_to(jnp.sum(picked, axis=1, keepdims=True), (ROWS, LANES))


def solve_coefficients(sums):
    order = len(sums)
    gram = [[sums[row][column : column + 1] for column in range(row + 1)] for row in range(order)]
    target_side = [-sums[-1][RHS_AT + i : RHS_AT + i + 1] for i in range(order)]
    return least_squares(gram, target_side)


def vmem():
    return pl.BlockSpec(memory_space=pltpu.VMEM)


def fluid_call(
    places, add_up, messages, sums, rbf_blocks, traction, massive, shells, stream, last
):
    blocks, nodes, _ = rbf_blocks.shape
    rows_all = messages[-1].shape[0]
    chunks = 3 * nodes // LANES
    halves = nodes // LANES
    k = len(messages) - 1
    first_time = k == 0
    devices = rows_all // (chunks * shells if first_time else FORTH)
    rows_back = devices * (FORTH if first_time else BACK)
    apart = shells if first_time else 1
    over = 16 * apart
    n_sums = len(sums)
    group = next(n for n in (26, 16, 8, 4, 2, 1) if blocks % n == 0)
    lag = min(group, 13)
    steps = blocks // group
    pieces = [(at * group, group) for at in range(steps)]
    if blocks == 104:
        pieces = [(0, 26), (26, 39), (65, 39)]

    def body(*refs):
        refs = list(refs)
        place_ref = refs.pop(0)
        add_ref = None if first_time else refs.pop(0)
        slot_ref = refs.pop(0) if first_time else None
        message_refs = [refs.pop(0) for _ in range(k + 1)]
        sum_refs = [refs.pop(0) for _ in range(n_sums)]
        source_ref, traction_ref, mass_ref = refs.pop(0), refs.pop(0), refs.pop(0)
        sending_ref = refs.pop(0)
        load_ref = refs.pop(0) if last else None
        start_out = refs.pop(0) if first_time else None
        sums_out, coefs_out = (refs.pop(0), refs.pop(0)) if k else (None, None)
        shown_ref, result_ref = refs.pop(0), refs.pop(0)
        kept_ref = refs.pop(0) if last else None
        begun_ref = refs.pop(0) if first_time else None
        rbf_ref, landed = (refs.pop(0), refs.pop(0)) if stream else (source_ref, None)

        def piece(at):
            rows = pl.ds(*pieces[at])
            return pltpu.make_async_copy(source_ref.at[rows], rbf_ref.at[rows], landed.at[at])

        if stream:
            for at in range(len(pieces)):
                piece(at).start()

        weights = []
        if k:
            line = jnp.dot(
                add_ref[...], message_refs[-1][...], preferred_element_type=jnp.float32
            )
            fresh = spread_sums(line[:1])
            sums_out[...] = fresh
            coefs_out[...] = jnp.zeros_like(coefs_out)
            weights = [RELAX]
            if k >= 2:
                coefs = solve_coefficients([ref[...] for ref in sum_refs] + [fresh])
                for i, coef in enumerate(coefs):
                    coefs_out[i : i + 1, :] = coef
                weights = [None] + [1.0 + coef for coef in coefs]

        def show(at, carry):
            rows = pl.ds(pl.multiple_of(at * FOLD, FOLD), FOLD)
            shown = message_refs[0][rows, :].astype(jnp.float32)
            for weight, ref in zip(weights, message_refs[1:]):
                change = ref[rows, :].astype(jnp.float32)
                shown = shown + (change if weight is None else weight * change)
            shown_ref[rows, :] = shown
            return carry

        lax.fori_loop(0, rows_all // FOLD, show, 0)
        shown_ref[rows_all:, :] = jnp.zeros((over, LANES), jnp.float32)
        result_ref[...] = jnp.zeros_like(result_ref)
        if first_time:
            begun_ref[...] = jnp.zeros_like(begun_ref)

        def load_of(block):
            spot = place_ref[0, block]
            rows = [
                shown_ref[pl.ds(spot + half * apart, 8, stride=halves * apart), :]
                for half in range(halves)
            ]
            if first_time:
                again = place_ref[2, block]
                for half in range(halves):
                    begun_ref[pl.ds(again + half, 3, stride=halves), :] = rows[half][:3]
            shown = jnp.concatenate(rows, axis=1).astype(jnp.bfloat16)
            moved = lax.dot_general(
                shown, rbf_ref[block], (((1,), (1,)), ((), ())), preferred_element_type=jnp.float32
            )
            rows = pl.ds(pl.multiple_of(block * 8, 8), 8)
            load = (traction_ref[rows, :] - mass_ref[rows, :] * moved).astype(jnp.bfloat16)
            if last:
                for half in range(halves):
                    lanes = slice(half * LANES, (half + 1) * LANES)
                    kept_ref[half, rows, :] = load[:, lanes].astype(jnp.float32)
            return load

        def map_back(block, load):
            spot = place_ref[1, block]
            result = jnp.dot(load, rbf_ref[block], preferred_element_type=jnp.float32)
            for half in range(halves):
                result_ref[pl.ds(spot + half, 3, stride=halves), :] = result[
                    :3, half * LANES : (half + 1) * LANES
                ]

        def contract(first, amount, behind):
            loads = {}
            for inner in range(amount + behind):
                if inner < amount:
                    loads[inner] = load_of(first + inner)
                if inner >= behind:
                    map_back(first + inner - behind, loads.pop(inner - behind))

        def contract_group(at, carry):
            contract(at * group, group, lag)
            return carry

        if stream:
            for at, (first, amount) in enumerate(pieces):
                piece(at).wait()
                contract(first, amount, min(amount, lag))
        else:
            lax.fori_loop(0, steps, contract_group, 0)
        if first_time:
            start_out[...] = begun_ref[...].astype(jnp.bfloat16)
            result_ref[pl.ds(2 * chunks, devices, stride=FORTH), :] = slot_ref[...]
        sending_ref[...] = result_ref[...].astype(jnp.bfloat16)
        if last:
            for at in range(chunks):
                component, half = divmod(at, halves)
                load_ref[:, at * LANES : (at + 1) * LANES] = kept_ref[
                    half, pl.ds(component, blocks, stride=8), :
                ].astype(jnp.bfloat16)

    out_shape = [jax.ShapeDtypeStruct((rows_back, LANES), jnp.bfloat16)]
    if last:
        out_shape.append(jax.ShapeDtypeStruct((blocks, 3 * nodes), jnp.bfloat16))
    if first_time:
        out_shape.append(jax.ShapeDtypeStruct((devices * FORTH, LANES), jnp.bfloat16))
    if k:
        out_shape += [jax.ShapeDtypeStruct((ROWS, LANES), jnp.float32)] * 2
    scratch = [
        pltpu.VMEM((rows_all + over, LANES), jnp.float32),
        pltpu.VMEM((rows_back, LANES), jnp.float32),
    ]
    if last:
        scratch.append(pltpu.VMEM((halves, blocks * 8, LANES), jnp.float32))
    if first_time:
        scratch.append(pltpu.VMEM((devices * FORTH, LANES), jnp.float32))
    if stream:
        scratch += [
            pltpu.VMEM(rbf_blocks.shape, rbf_blocks.dtype),
            pltpu.SemaphoreType.DMA((len(pieces),)),
        ]
    inputs = (add_up, *messages, *sums, rbf_blocks, traction, massive)
    in_specs = [vmem()] * len(inputs)
    if stream:
        rbf_blocks = pltpu.with_memory_space_constraint(rbf_blocks, pltpu.HBM)
        inputs = (add_up, *messages, *sums, rbf_blocks, traction, massive)
        in_specs[-3] = pl.BlockSpec(memory_space=pltpu.HBM)
    out = pl.pallas_call(
        body,
        in_specs=[pl.BlockSpec(memory_space=pltpu.SMEM)] + in_specs,
        out_specs=[vmem()] * len(out_shape),
        out_shape=out_shape,
        scratch_shapes=scratch,
        compiler_params=pltpu.CompilerParams(
            vmem_limit_bytes=STREAM_LIMIT if stream else SMALL_LIMIT
        ),
        name="fluid_side",
    )(places, *inputs)
    out = list(out)
    sending = out.pop(0)
    if first_time:
        return sending, out[0]
    load = out.pop(0) if last else None
    return sending, load, *out


def full_sum(array):
    return jnp.sum(jnp.sum(array, axis=0, keepdims=True), axis=1, keepdims=True)


def shell_call(
    arrived,
    coefs,
    shown,
    residuals,
    images,
    start,
    robin_coef,
    collect,
    pick,
    shell_inverse,
    stream,
    last,
):
    shells, breadth, _ = shell_inverse.shape
    chunks = breadth // LANES
    height = chunks * shells
    k = len(images)

    def body(*refs):
        refs = list(refs)
        arrived_ref = refs.pop(0)
        coef_ref = refs.pop(0) if k else None
        shown_ref = refs.pop(0)
        residual_refs = [refs.pop(0) for _ in range(k)]
        image_refs = [refs.pop(0) for _ in range(k)]
        start_ref, robin_ref, collect_ref, pick_ref, inverse_ref = [refs.pop(0) for _ in range(5)]
        message_ref, image_out = refs.pop(0), refs.pop(0)
        residual_out, shown_out = (None, None) if last else (refs.pop(0), refs.pop(0))
        near_ref, landed = refs if stream else (inverse_ref, None)
        copies = []
        if stream:
            for s in range(shells):
                copies.append(
                    pltpu.make_async_copy(inverse_ref.at[s], near_ref.at[s], landed.at[s])
                )
                copies[-1].start()

        load = jnp.dot(collect_ref[...], arrived_ref[...], preferred_element_type=jnp.float32)
        if k == 0:
            current = start_ref[...]
        elif k == 1:
            current = start_ref[...] + RELAX * residual_refs[0][...]
        else:
            current = image_refs[-1][...]
            for i in range(k - 1):
                current = current + coef_ref[i : i + 1, :] * (
                    image_refs[i + 1][...] - image_refs[i][...]
                )
        forcing = load + robin_ref[...] * current
        forcing = jnp.concatenate(
            [forcing[t * shells : (t + 1) * shells] for t in range(chunks)], axis=1
        ).astype(jnp.bfloat16)
        row = lax.broadcasted_iota(jnp.int32, (shells, breadth), 0)

        wide = jnp.zeros((shells, breadth), jnp.float32)
        for s in range(shells):
            if stream:
                copies[s].wait()
            product = jnp.dot(forcing, near_ref[s], preferred_element_type=jnp.float32)
            wide = jnp.where(row == s, product, wide)
        image = jnp.concatenate([wide[:, t * LANES : (t + 1) * LANES] for t in range(chunks)], axis=0)
        image_out[...] = image
        residual = image - current
        lane = lax.broadcasted_iota(jnp.int32, (1, LANES), 1)
        line = jnp.where(lane == SQUARES_AT, full_sum(residual * residual), 0.0)
        if k:
            chain = [ref[...] for ref in residual_refs] + [residual]
            changes = [chain[i + 1] - chain[i] for i in range(k)]
            for i, change in enumerate(changes):
                line = line + jnp.where(lane == i, full_sum(changes[-1] * change), 0.0)
                line = line + jnp.where(lane == RHS_AT + i, full_sum(change * residual), 0.0)
        head = line.astype(jnp.bfloat16).astype(jnp.float32)
        rest = line - head
        middle = rest.astype(jnp.bfloat16).astype(jnp.float32)
        tail = (rest - middle).astype(jnp.bfloat16).astype(jnp.float32)
        pieces = head + pltpu.roll(middle, PIECE, 1) + pltpu.roll(tail, 2 * PIECE, 1)
        if last:
            message_ref[...] = jnp.broadcast_to(pieces, message_ref.shape).astype(jnp.bfloat16)
            return
        residual_out[...] = residual
        difference = (image - shown_ref[...]).astype(jnp.bfloat16)
        shown_out[...] = shown_ref[...] + difference.astype(jnp.float32)
        first = lax.broadcasted_iota(jnp.int32, (ROWS, LANES), 0) == 0
        below = jnp.where(first, jnp.broadcast_to(pieces, (ROWS, LANES)), 0.0).astype(jnp.bfloat16)
        message_ref[...] = jnp.dot(
            pick_ref[...],
            jnp.concatenate([difference, below], axis=0),
            preferred_element_type=jnp.float32,
        ).astype(jnp.bfloat16)

    inputs = (
        [arrived]
        + ([coefs] if k else [])
        + [shown, *residuals, *images, start, robin_coef, collect, pick, shell_inverse]
    )
    own = jax.ShapeDtypeStruct((height, LANES), jnp.float32)
    if last:
        out_shape = [jax.ShapeDtypeStruct((ROWS, LANES), jnp.bfloat16), own]
    else:
        rows_out = pick.shape[0]
        out_shape = [jax.ShapeDtypeStruct((rows_out, LANES), jnp.bfloat16), own, own, own]
    in_specs = [vmem()] * len(inputs)
    scratch = []
    if stream:
        inputs[-1] = pltpu.with_memory_space_constraint(shell_inverse, pltpu.HBM)
        in_specs[-1] = pl.BlockSpec(memory_space=pltpu.HBM)
        scratch = [
            pltpu.VMEM(shell_inverse.shape, shell_inverse.dtype),
            pltpu.SemaphoreType.DMA((shells,)),
        ]
    return pl.pallas_call(
        body,
        in_specs=in_specs,
        out_specs=[vmem()] * len(out_shape),
        out_shape=out_shape,
        scratch_shapes=scratch,
        compiler_params=pltpu.CompilerParams(
            vmem_limit_bytes=STREAM_LIMIT if stream else SMALL_LIMIT
        ),
        name="shell_side",
    )(*inputs)


def closing_call(ending, sums, images, shells, count):
    height = images[0].shape[0]
    chunks = height // shells
    n_sums = len(sums)

    def body(*refs):
        refs = list(refs)
        ending_ref = refs.pop(0)
        sum_refs = [refs.pop(0) for _ in range(n_sums)]
        image_refs = [refs.pop(0) for _ in range(len(images))]
        current_ref, norm_ref = refs
        pieces = jnp.sum(ending_ref[...].astype(jnp.float32), axis=0, keepdims=True)
        fresh = spread_sums(pieces * 0.5)
        every = [ref[...] for ref in sum_refs] + [fresh]
        coefs = solve_coefficients(every[1:])
        moving = image_refs[-1][...]
        for i, coef in enumerate(coefs):
            moving = moving + coef * (image_refs[i + 1][...] - image_refs[i][...])
        for t in range(chunks):
            current_ref[:, t * LANES : (t + 1) * LANES] = moving[t * shells : (t + 1) * shells]
        for i, part in enumerate(every):
            norm = jnp.sqrt(part[SQUARES_AT : SQUARES_AT + 1] / count + EPSILON)
            norm_ref[i] = norm[0, 0]

    return pl.pallas_call(
        body,
        in_specs=[vmem()] * (1 + n_sums + len(images)),
        out_specs=[vmem(), pl.BlockSpec(memory_space=pltpu.SMEM)],
        out_shape=[
            jax.ShapeDtypeStruct((shells, chunks * LANES), jnp.float32),
            jax.ShapeDtypeStruct((n_sums + 1,), jnp.float32),
        ],
        name="closing",
    )(ending, *sums, *images)


def spread_components(array, blocks, nodes):
    wide = array.astype(jnp.float32).reshape(blocks, 3, nodes)
    return jnp.pad(wide, ((0, 0), (0, 5), (0, 0))).reshape(blocks * 8, nodes)


def by_chunks(array, shells):
    return array.reshape(shells, -1, LANES).transpose(1, 0, 2).reshape(-1, LANES)


def per_device(
    rbf_blocks, fluid_traction, fluid_mass, route, slot, shell_inverse, robin_coef, shell_start
):
    devices = lax.axis_size(FLUID) * lax.axis_size("solid")
    blocks = rbf_blocks.shape[0]
    nodes = rbf_blocks.shape[1]
    breadth = 3 * nodes
    chunks = breadth // LANES
    shells = shell_inverse.shape[0]
    height = chunks * shells
    capacity = 2
    count = shells * devices * breadth

    def exchange(array):
        return lax.all_to_all(array, FLUID_SOLID, split_axis=0, concat_axis=0, tiled=True)

    def transport(buffer, part):
        moved = exchange(buffer.reshape(devices, -1, part, LANES))
        return moved.reshape(-1, LANES)

    start = by_chunks(shell_start, shells)
    start_half = start.astype(jnp.bfloat16)

    destination = route[:, 0]
    block_order = jnp.arange(blocks, dtype=jnp.int32)
    earlier = (destination[:, None] == destination[None, :]) & (
        block_order[None, :] < block_order[:, None]
    )
    slot_rank = jnp.sum(earlier.astype(jnp.int32), axis=1)
    places = jnp.stack(
        [destination * FORTH + slot_rank * chunks, destination * BACK + slot_rank * chunks]
    )
    solid = lax.axis_size("solid")
    upper = destination // solid
    begun_from = upper % 2 * (devices // 2) + upper // 2 * solid + destination % solid
    first_places = jnp.stack(
        [
            begun_from * height + slot,
            destination * FORTH + slot_rank * chunks,
            destination * FORTH + slot_rank * chunks,
        ]
    )
    peers = jnp.arange(devices, dtype=jnp.int32)
    lanes = jnp.arange(LANES, dtype=jnp.int32)
    wanted = jnp.where(slot_rank[:, None] == lanes[None, :], slot[:, None] + 1, 0)
    asking = jnp.dot(
        (peers[:, None] == destination[None, :]).astype(jnp.bfloat16),
        wanted.astype(jnp.bfloat16),
        preferred_element_type=jnp.float32,
    )

    traction = spread_components(fluid_traction, blocks, nodes)
    massive = spread_components(fluid_mass, blocks, nodes)
    robin = by_chunks(robin_coef, shells)

    shown = start_half.astype(jnp.float32)
    stacked = jnp.arange(height + ROWS, dtype=jnp.int32)
    summed = jnp.arange(devices * FORTH, dtype=jnp.int32)[None, :] % FORTH == capacity * chunks
    add_up = jnp.broadcast_to(summed, (ROWS, devices * FORTH)).astype(jnp.bfloat16)

    def one_hot(asked):
        order = jnp.arange(FORTH, dtype=jnp.int32)[None, :]
        named = jnp.where(order < chunks, asked[:, :1], asked[:, 1:2])
        rows = jnp.where(
            (named >= 0) & (order < capacity * chunks), (order % chunks) * shells + named, -1
        )
        forth = jnp.where(order == capacity * chunks, height, rows).reshape(-1)
        pick = (forth[:, None] == stacked[None, :]).astype(jnp.bfloat16)
        collect_first = (stacked[:height, None] == rows.reshape(-1)[None, :]).astype(jnp.bfloat16)
        back = rows[:, :BACK].reshape(-1)
        collect = (stacked[:height, None] == back[None, :]).astype(jnp.bfloat16)
        return pick, collect_first, collect

    begun = start_half
    for axes, amount in ((("fluid_0", "fluid_1", "solid"), devices // 2), (("fluid_2",), 2)):
        begun = lax.all_to_all(
            jnp.broadcast_to(begun[None], (amount, *begun.shape)),
            axes,
            split_axis=0,
            concat_axis=0,
            tiled=True,
        ).reshape(-1, LANES)
    messages = []
    sums = []
    residuals = []
    images = []
    last_load = None
    for iteration in range(ITERS):
        last = iteration == ITERS - 1
        coefs = None
        if iteration == 0:
            sending, message = fluid_call(
                first_places, asking, [begun], [], rbf_blocks, traction, massive, shells, True, last
            )
            arrived = transport(sending, 2)
            rows = jnp.arange(devices * FORTH, dtype=jnp.int32)[None, :]
            numbers = peers[:, None] * FORTH + capacity * chunks == rows
            asked = jnp.dot(
                numbers.astype(jnp.bfloat16), arrived, preferred_element_type=jnp.float32
            )
            pick, collect_now, collect = one_hot(asked.astype(jnp.int32) - 1)
            pick, collect_now, collect, add_up, places, arrived = lax.optimization_barrier(
                (pick, collect_now, collect, add_up, places, arrived)
            )
        else:
            message = transport(outgoing, 2)
        messages.append(message)
        if iteration:
            sending, last_load, fresh, coefs = fluid_call(
                places,
                add_up,
                messages,
                sums[1:],
                rbf_blocks,
                traction,
                massive,
                shells,
                iteration < FLUID_STREAMS,
                last,
            )
            sums.append(fresh)
            arrived = transport(sending, 4)
            collect_now = collect
        made = shell_call(
            arrived,
            coefs,
            shown,
            residuals,
            images,
            start,
            robin,
            collect_now,
            pick,
            shell_inverse,
            iteration < SHELL_STREAMS,
            last,
        )
        outgoing, image = made[:2]
        images.append(image)
        if not last:
            residuals.append(made[2])
            shown = made[3]
    ending = transport(jnp.broadcast_to(outgoing[:1], (devices * 2, LANES)), 2)
    current, norms = closing_call(ending, sums, images, shells, count)
    return (current, last_load, norms)


def solution(mesh):
    split = Mesh(
        mesh.devices.reshape(4, 4, 2, mesh.shape["solid"]),
        ("fluid_0", "fluid_1", "fluid_2", "solid"),
    )
    placed = (
        P(FLUID_SOLID, None, None),
        P(FLUID_SOLID, None),
        P(FLUID_SOLID, None),
        P(FLUID_SOLID, None),
        P(FLUID_SOLID),
        P(FLUID_SOLID, None, None),
        P(FLUID_SOLID, None),
        P(FLUID_SOLID, None),
    )
    return jax.shard_map(
        per_device,
        mesh=split,
        in_specs=placed,
        out_specs=(P(FLUID_SOLID, None), P(FLUID_SOLID, None), P()),
        check_vma=False,
    )
```
